128 devices in a mesh: section: 16 (over x_hi, y, core), expert: 8 (over z, x_lo).
Axes of the slice: x: 4 (x_hi: 2, x_lo: 2; x = x_hi * 2 + x_lo), y: 4, z: 4, core: 2. Of those that a mesh axis runs over, the one named last changes fastest.
Arguments:
- fwd_input: bfloat16 [16, 1024, 2560], P('section', 'expert'), may hold values from -6 to 6
- back_input: bfloat16 [16, 1024, 2560], P('section', 'expert'), may hold values from -6 to 6
- cot_input: bfloat16 [16, 1024, 2560], P('section', 'expert'), may hold values from -6 to 6
- fwd_routes: int32 [16, 1024, 2], P('section', 'expert'), may hold values from 0 to 7, all different within a row; in each aligned block of 128 rows (0 to 127, 128 to 255, ..., all dimensions but the last counted through in order) at most 64 rows name the same one
- back_routes: int32 [16, 1024, 2], P('section', 'expert'), may hold values from 0 to 7, all different within a row; in each aligned block of 128 rows (0 to 127, 128 to 255, ..., all dimensions but the last counted through in order) at most 64 rows name the same one
- fwd_gates: float32 [16, 1024, 2], P('section', 'expert'), may hold values from 0.05 to 1
- back_gates: float32 [16, 1024, 2], P('section', 'expert'), may hold values from 0.05 to 1
- w_gate: bfloat16 [16, 8, 2560, 768], P('section', 'expert'), may hold values from -0.125 to 0.125
- w_up: bfloat16 [16, 8, 2560, 768], P('section', 'expert'), may hold values from -0.125 to 0.125
- w_down: bfloat16 [16, 8, 768, 2560], P('section', 'expert'), may hold values from -0.21875 to 0.21875
- norm_gain: float32 [16, 2560], P('section'), may hold values from 0.1 to 1.9
- verdict_head: float32 [2560], replicated, may hold values from -0.125 to 0.125
- verdict_labels: int32 [1024], P('expert'), may hold values from 0 to 1
Outputs:
- next_input: bfloat16 [16, 1024, 2560], P('section', 'expert')
- prev_grad: bfloat16 [16, 1024, 2560], P('section', 'expert')
- gain_grad: float32 [16, 2560], P('section')
- grad_gate: bfloat16 [16, 8, 2560, 768], P('section', 'expert')
- grad_up: bfloat16 [16, 8, 2560, 768], P('section', 'expert')
- grad_down: bfloat16 [16, 8, 768, 2560], P('section', 'expert')
The draws below stay inside these ranges and needn't reach their ends.
Inputs may be any that keep to these rules, and one draw needn't show every extreme that they name: `fwd_routes`: each row names 2 different experts; within the rows of one device no expert is named by more than 64 rows, a bound that some block reaches. `back_routes`: as for fwd_routes.
All inputs are finite; a program needn't handle non-finite values.
Results may differ from the reference program's by a relative error of at most 0.012.
Values may be sent and summed in bfloat16 or wider, within the bound.
No kernel may reach another device: no remote copies, remote signals or barrier semaphores. Data moves between devices by JAX's collectives and lax.ppermute only.
A program may use at most 128 MiB of HBM per device.

```python
import math
import jax
import jax.numpy as jnp
import numpy as np
from jax import lax

D = 2560
HID = 768
TOP = 2
TOK_DEV = 128
EXPERTS = 8
SECTIONS = 16
TOKENS = 1024
MOST = 64
N_EXPERT = 8


def set_ends(result, key, low, largest):
    longest = result.shape.index(max(result.shape))
    spots = []
    for shift in (0, 1):
        where = [jax.random.randint(jax.random.fold_in(key, axis), (), 0, length) for axis, length in enumerate(result.shape)]
        where[longest] = (where[longest] + shift) % result.shape[longest]
        spots.append(tuple(where))
    return result.at[spots[0]].set(low).at[spots[1]].set(largest)


def block_levels(rng, dims, pieces, low, largest):
    level = 1.0
    for axis_at, shards_of in pieces:
        draws = jax.random.uniform(jax.random.fold_in(jax.random.fold_in(rng, 6), axis_at), (shards_of,), jnp.float32, low / len(pieces), largest / len(pieces))
        level = level * jnp.repeat(jnp.exp(draws), dims[axis_at] // shards_of).reshape((-1,) + (1,) * (len(dims) - 1 - axis_at))
    return level


def shared_out(rng, own, number, rows, amount, top, limit, slope):
    order = jax.random.permutation(rng, amount)
    crowded, common = shares(amount, rows * top, limit, slope, True), shares(amount, rows * top, limit, slope, False)
    places = jnp.arange(amount)

    def named(lengths, rotation):
        used = int((lengths > 0).sum())
        fixed = max(1, used // 4)
        moved = fixed + (places - fixed + rotation * (used - fixed)) % max(1, amount - fixed)
        return jnp.zeros((amount,), jnp.int32).at[order[jnp.where(places < fixed, places, moved)]].set(jnp.asarray(lengths, jnp.int32))

    lengths = jnp.where(number % 4 == 0, named(crowded, number // 4), named(common, number - number // 4 - 1))
    mixed = jax.random.permutation(jax.random.fold_in(own, 3), amount)
    giver, sink = mixed[0:amount // 2 * 2:2], mixed[1:amount // 2 * 2:2]
    slack = jnp.minimum(lengths[giver] - 1, limit - lengths[sink]) // 2
    slack = jnp.where((giver == order[0]) | (sink == order[0]) | (lengths[sink] == 0), 0, jnp.maximum(slack, 0))
    moved = jax.random.randint(jax.random.fold_in(own, 4), (amount // 2,), 0, 1 << 20) % (slack + 1)
    lengths = lengths.at[giver].add(-moved).at[sink].add(moved)
    labels = jnp.searchsorted(jnp.cumsum(lengths), jnp.arange(rows * top), side="right").astype(jnp.int32)
    listing = labels.reshape(top, rows).T
    listing = listing[jax.random.permutation(jax.random.fold_in(own, 1), rows)]
    rotation = jax.random.randint(jax.random.fold_in(own, 2), (rows, 1), 0, top)
    return jnp.take_along_axis(listing, (jnp.arange(top)[None, :] + rotation) % top, axis=1)


def shares(count, total, bound, slope, full):
    weights = [(1 << 20) // math.isqrt(rank ** slope) + 1 for rank in range(1, count + 1)]
    largest = bound if full else min(bound, max(-(-total // count), total * weights[0] // sum(weights)))
    least = 1 if total - largest >= count - 1 else 0
    given, surplus = [largest] + [least] * (count - 1), total - largest - least * (count - 1)
    while surplus > 0:
        movable = [i for i in range(1, count) if given[i] < largest] or [i for i in range(1, count) if given[i] < bound]
        whole, left = sum([weights[i] for i in movable]), surplus
        for i in movable:
            extra = min(bound - given[i], max(1, left * weights[i] // whole), surplus)
            given[i] = given[i] + extra
            surplus = surplus - extra
    return np.array(given)


def scatter_about(own_key, extent, scale, most, shards=(), kind=jnp.bfloat16):
    gain = block_levels(own_key, extent, shards, -0.22, 0.18) if shards else 1.0
    result = jax.random.normal(own_key, extent, jnp.float32) * scale * gain
    return jnp.minimum(jnp.maximum(result, -most), most).astype(kind)


def setup_inputs(seed: int = 0) -> dict:
    key_list = jax.random.split(jax.random.key(seed), 14)
    fwd_input = scatter_about(key_list[0], (SECTIONS, TOKENS, D), 1.0, 6.0, ((0, 16), (1, 8)))
    back_input = scatter_about(key_list[1], (SECTIONS, TOKENS, D), 1.0, 6.0, ((0, 16), (1, 8)))
    cot_input = scatter_about(key_list[2], (SECTIONS, TOKENS, D), 1.0, 6.0, ((0, 16), (1, 8)))
    fwd_routes_keys = jax.random.split(jax.random.fold_in(key_list[3], 1), SECTIONS * TOKENS // TOK_DEV)
    fwd_routes_turns = jax.random.permutation(jax.random.fold_in(key_list[3], 3), SECTIONS * TOKENS // TOK_DEV)
    fwd_routes = jax.vmap(lambda own, number: shared_out(jax.random.fold_in(key_list[3], 2), own, number, TOK_DEV, EXPERTS, TOP, MOST, 2))(fwd_routes_keys, fwd_routes_turns).reshape((SECTIONS, TOKENS, TOP))
    back_routes_keys = jax.random.split(jax.random.fold_in(key_list[4], 1), SECTIONS * TOKENS // TOK_DEV)
    back_routes_turns = jax.random.permutation(jax.random.fold_in(key_list[4], 3), SECTIONS * TOKENS // TOK_DEV)
    back_routes = jax.vmap(lambda own, number: shared_out(jax.random.fold_in(key_list[4], 2), own, number, TOK_DEV, EXPERTS, TOP, MOST, 2))(back_routes_keys, back_routes_turns).reshape((SECTIONS, TOKENS, TOP))
    fwd_gates = jnp.clip(jnp.exp(math.log(1.0) - 2.9957323 * jax.random.uniform(key_list[5], (SECTIONS, TOKENS, TOP), jnp.float32) ** block_levels(key_list[5], (SECTIONS, TOKENS, TOP), ((0, 16), (1, 8)), -0.2, 0.2)), 0.05, 1.0)
    back_gates = jnp.clip(jnp.exp(math.log(1.0) - 2.9957323 * jax.random.uniform(key_list[6], (SECTIONS, TOKENS, TOP), jnp.float32) ** block_levels(key_list[6], (SECTIONS, TOKENS, TOP), ((0, 16), (1, 8)), -0.2, 0.2)), 0.05, 1.0)
    w_gate = scatter_about(key_list[7], (SECTIONS, EXPERTS, D, HID), D ** -0.5, 0.125, ((0, 16), (1, 8)))
    w_up = scatter_about(key_list[8], (SECTIONS, EXPERTS, D, HID), D ** -0.5, 0.125, ((0, 16), (1, 8)))
    w_down = scatter_about(key_list[9], (SECTIONS, EXPERTS, HID, D), HID ** -0.5, 0.21875, ((0, 16), (1, 8)))
    norm_gain = jnp.clip(1.0 + 0.18 * jax.random.normal(key_list[10], (SECTIONS, D), jnp.float32), 0.1, 1.9)
    verdict_head = scatter_about(key_list[11], (D,), D ** -0.5, 0.125, (), jnp.float32)
    verdict_labels = set_ends(jax.random.randint(key_list[12], (TOKENS,), 0, 2), jax.random.fold_in(key_list[12], 1), 0, 1).astype(jnp.int32)
    return {"fwd_input": fwd_input, "back_input": back_input, "cot_input": cot_input, "fwd_routes": fwd_routes, "back_routes": back_routes, "fwd_gates": fwd_gates, "back_gates": back_gates, "w_gate": w_gate, "w_up": w_up, "w_down": w_down, "norm_gain": norm_gain, "verdict_head": verdict_head, "verdict_labels": verdict_labels}


loss_scale = 64.0
norm_eps = 1e-06

def normalize(inputs, gain_row):
    mean_square = lax.optimization_barrier(jnp.mean(inputs * inputs, axis=-1, keepdims=True))
    inv_rms = lax.rsqrt(mean_square + norm_eps)
    return (inv_rms, (inputs * inv_rms * gain_row).astype(jnp.bfloat16))

def contract_rows(left_op, right_op):
    return lax.dot_general(left_op, right_op, (((0,), (0,)), ((), ())), preferred_element_type=jnp.float32)

def contract_cols(left_op, right_op):
    return lax.dot_general(left_op, right_op, (((1,), (1,)), ((), ())), preferred_element_type=jnp.float32)

def expert_forward(in_rows, w_gate, w_up, w_down):
    gate_pre = jnp.dot(in_rows, w_gate, preferred_element_type=jnp.float32)
    up_pre = jnp.dot(in_rows, w_up, preferred_element_type=jnp.float32)
    hidden = (jax.nn.silu(gate_pre) * up_pre).astype(jnp.bfloat16)
    return jnp.dot(hidden, w_down, preferred_element_type=jnp.float32).astype(jnp.bfloat16)

def expert_backward(in_rows, d_outs, w_gate, w_up, w_down):
    gate_pre = jnp.dot(in_rows, w_gate, preferred_element_type=jnp.float32)
    up_pre = jnp.dot(in_rows, w_up, preferred_element_type=jnp.float32)
    gate_sigmoid = jax.nn.sigmoid(gate_pre)
    gate_silu = gate_pre * gate_sigmoid
    hidden = (gate_silu * up_pre).astype(jnp.bfloat16)
    grad_d = contract_rows(hidden, d_outs)
    d_hidden = contract_cols(d_outs, w_down)
    d_gate = (d_hidden * up_pre * gate_sigmoid * (1.0 + gate_pre * (1.0 - gate_sigmoid))).astype(jnp.bfloat16)
    d_up = (d_hidden * gate_silu).astype(jnp.bfloat16)
    grad_g = contract_rows(in_rows, d_gate)
    grad_u = contract_rows(in_rows, d_up)
    d_rows = (contract_cols(d_gate, w_gate) + contract_cols(d_up, w_up)).astype(jnp.bfloat16)
    return (d_rows, grad_g, grad_u, grad_d)

def route_slots(flat_ids, expert_id, capacity):
    hit_mask = flat_ids == expert_id
    slot_rows = jnp.nonzero(hit_mask, size=capacity, fill_value=0)[0].astype(jnp.int32)
    filled = jnp.arange(capacity, dtype=jnp.int32) < jnp.sum(hit_mask.astype(jnp.int32))
    return (slot_rows, filled)

def section_pass(section_index, fwd_x, back_x, cot_in, fwd_ids, back_ids, fwd_weight, back_weight, gate_all, up_all, down_all, gain_row, verdict_head, verdict_labels):
    capacity = N_EXPERT * MOST
    expert_ids = jnp.arange(EXPERTS, dtype=jnp.int32)
    x_fwd = fwd_x.astype(jnp.float32)
    inv_fwd, normed_fwd = normalize(x_fwd, gain_row)
    ids_fwd = fwd_ids.reshape(-1)
    mix_fwd = fwd_weight.reshape(-1)

    def forward_expert(mixed_sum, packed):
        expert_id, w_gate, w_up, w_down = packed
        slot_rows, filled = route_slots(ids_fwd, expert_id, capacity)
        token_rows = slot_rows // TOP
        expert_out = expert_forward(normed_fwd[token_rows], w_gate, w_up, w_down)
        scale_rows = jnp.where(filled, mix_fwd[slot_rows], 0.0)
        return (mixed_sum.at[token_rows].add(expert_out.astype(jnp.float32) * scale_rows[:, None]), None)
    mixed_sum, unused = lax.scan(forward_expert, jnp.zeros(x_fwd.shape, jnp.float32), (expert_ids, gate_all, up_all, down_all))
    layer_out = (x_fwd + mixed_sum).astype(jnp.bfloat16)
    logits = lax.optimization_barrier(jnp.sum(layer_out.astype(jnp.float32) * verdict_head[None, :], axis=-1))
    last_cot = loss_scale * (jax.nn.sigmoid(logits) - verdict_labels.astype(jnp.float32))[:, None] * verdict_head[None, :]
    is_last = section_index == SECTIONS - 1
    x_back = jnp.where(is_last, fwd_x, back_x).astype(jnp.float32)
    ids_back = jnp.where(is_last, fwd_ids, back_ids).reshape(-1)
    mix_back = jnp.where(is_last, fwd_weight, back_weight).reshape(-1)
    cotangent = jnp.where(is_last, last_cot, cot_in.astype(jnp.float32))
    inv_back, normed_back = normalize(x_back, gain_row)

    def backward_expert(d_normed, packed):
        expert_id, w_gate, w_up, w_down = packed
        slot_rows, filled = route_slots(ids_back, expert_id, capacity)
        token_rows = slot_rows // TOP
        d_outs = jnp.where(filled[:, None], mix_back[slot_rows][:, None] * cotangent[token_rows], 0.0).astype(jnp.bfloat16)
        d_rows, grad_g, grad_u, grad_d = expert_backward(normed_back[token_rows], d_outs, w_gate, w_up, w_down)
        d_normed = d_normed.at[token_rows].add(jnp.where(filled[:, None], d_rows.astype(jnp.float32), 0.0))
        return (d_normed, (grad_g.astype(jnp.bfloat16), grad_u.astype(jnp.bfloat16), grad_d.astype(jnp.bfloat16)))
    d_normed, grads = lax.scan(backward_expert, jnp.zeros(x_back.shape, jnp.float32), (expert_ids, gate_all, up_all, down_all))
    scaled = gain_row * d_normed
    inv_cube = inv_back * inv_back * inv_back
    d_input = cotangent + inv_back * scaled - x_back * inv_cube * lax.optimization_barrier(jnp.mean(x_back * scaled, axis=-1, keepdims=True))
    gain_grad = lax.optimization_barrier(jnp.sum(d_normed * x_back * inv_back, axis=0))
    return (layer_out, d_input.astype(jnp.bfloat16), gain_grad, grads[0], grads[1], grads[2])

def reference(fwd_input, back_input, cot_input, fwd_routes, back_routes, fwd_gates, back_gates, w_gate, w_up, w_down, norm_gain, verdict_head, verdict_labels):

    def run_section(packed):
        return section_pass(*packed, verdict_head, verdict_labels)
    section_ids = jnp.arange(SECTIONS, dtype=jnp.int32)
    layer_out, d_input, gain_grad, grad_gate, grad_up, grad_down = lax.map(run_section, (section_ids, fwd_input, back_input, cot_input, fwd_routes, back_routes, fwd_gates, back_gates, w_gate, w_up, w_down, norm_gain))
    next_input = jnp.concatenate([jnp.zeros_like(layer_out[:1]), layer_out[:-1]], axis=0)
    prev_grad = jnp.concatenate([d_input[1:], jnp.zeros_like(d_input[:1])], axis=0)
    return (next_input, prev_grad, gain_grad, grad_gate, grad_up, grad_down)
```

```python
import jax
import jax.numpy as jnp
from jax import lax
from jax.experimental import pallas as pl
from jax.experimental.pallas import tpu as pltpu
from jax.sharding import PartitionSpec as P

loss_scale = 64.0
norm_eps = 1e-06
bf16 = jnp.bfloat16
f32 = jnp.float32
chunk = 512
vmem = pl.BlockSpec(memory_space=pltpu.VMEM)
smem = pl.BlockSpec(memory_space=pltpu.SMEM)


def passed_along(value, axis, steps):
    count = lax.axis_size(axis)
    initial, last = (max(0, -steps), min(count, count - steps))
    return lax.ppermute(value, axis, [(source, source + steps) for source in range(initial, last)])


def slot_keys(ids, groups, capacity):
    tokens = ids.shape[0]
    lanes = lax.broadcasted_iota(jnp.int32, (tokens, 128), 1)
    hit0 = ids[:, 0:1] == lanes
    hit1 = ids[:, 1:2] == lanes
    hits = (hit0 | hit1).astype(bf16)
    before = (
        lax.broadcasted_iota(jnp.int32, (tokens, tokens), 1)
        < lax.broadcasted_iota(jnp.int32, (tokens, tokens), 0)
    ).astype(bf16)
    ranks = jnp.dot(before, hits, preferred_element_type=f32)
    rank0 = jnp.sum(jnp.where(hit0, ranks, 0.0), axis=1, keepdims=True).astype(jnp.int32)
    rank1 = jnp.sum(jnp.where(hit1, ranks, 0.0), axis=1, keepdims=True).astype(jnp.int32)
    return ids[:, 0:1] * capacity + rank0, ids[:, 1:2] * capacity + rank1


def slot_hits(ids, groups, capacity):
    key0, key1 = slot_keys(ids, groups, capacity)
    slots = lax.broadcasted_iota(jnp.int32, (ids.shape[0], groups * capacity), 1)
    return key0 == slots, key1 == slots


def split_weights(hit0, hit1, gates):
    weights = jnp.where(hit0, gates[:, 0:1], 0.0) + jnp.where(hit1, gates[:, 1:2], 0.0)
    high = weights.astype(bf16)
    low = (weights - high.astype(f32)).astype(bf16)
    return high, low


def over_tokens(left, right):
    return lax.dot_general(left, right, (((0,), (0,)), ((), ())), preferred_element_type=f32)


def inv_rms_of(rows):
    return lax.rsqrt(jnp.mean(rows * rows, axis=-1, keepdims=True) + norm_eps)


def chunks(width):
    return [slice(at, min(at + chunk, width)) for at in range(0, width, chunk)]


def send_forward(groups, capacity, x_ref, gain_ref, ids_ref, out_ref):
    hit0, hit1 = slot_hits(ids_ref[...], groups, capacity)
    pick = (hit0 | hit1).astype(bf16)
    x = x_ref[...].astype(f32)
    normed = (x * inv_rms_of(x) * gain_ref[...]).astype(bf16)
    for cols in chunks(x.shape[1]):
        out_ref[:, cols] = over_tokens(pick, normed[:, cols]).astype(bf16)


def send_backward(
    groups,
    capacity,
    last_ref,
    fwd_ref,
    back_ref,
    cot_ref,
    gain_ref,
    head_ref,
    fwd_ids_ref,
    back_ids_ref,
    fwd_gates_ref,
    back_gates_ref,
    rows_ref,
    dout_ref,
):
    is_last = last_ref[0] == 1
    ids = jnp.where(is_last, fwd_ids_ref[...], back_ids_ref[...])
    gates = jnp.where(is_last, fwd_gates_ref[...], back_gates_ref[...])
    hit0, hit1 = slot_hits(ids, groups, capacity)
    pick = (hit0 | hit1).astype(bf16)
    high, low = split_weights(hit0, hit1, gates)
    x = jnp.where(is_last, fwd_ref[...].astype(f32), back_ref[...].astype(f32))
    normed = (x * inv_rms_of(x) * gain_ref[...]).astype(bf16)
    for cols in chunks(x.shape[1]):
        rows_ref[:, cols] = over_tokens(pick, normed[:, cols]).astype(bf16)
        cot = cot_ref[:, cols]
        head = jnp.broadcast_to(head_ref[:, cols], cot.shape)
        head_high = head.astype(bf16)
        head_low = (head - head_high.astype(f32)).astype(bf16)
        cot_high = jnp.where(is_last, head_high.astype(f32), cot.astype(f32)).astype(bf16)
        cot_low = jnp.where(is_last, head_low.astype(f32), 0.0).astype(bf16)
        dout_ref[:, cols] = (
            over_tokens(high, cot_high) + over_tokens(low, cot_high) + over_tokens(high, cot_low)
        ).astype(bf16)


def join_forward(
    groups,
    capacity,
    last_ref,
    ret_ref,
    x_ref,
    ids_ref,
    gates_ref,
    head_ref,
    labels_ref,
    out_ref,
    coef_ref,
    slots_ref,
):
    is_last = last_ref[0] == 1
    hit0, hit1 = slot_hits(ids_ref[...], groups, capacity)
    high, low = split_weights(hit0, hit1, gates_ref[...])
    logits = jnp.zeros((x_ref.shape[0], 1), f32)
    for cols in chunks(x_ref.shape[1]):
        ret = ret_ref[:, cols]
        mixed = jnp.dot(high, ret, preferred_element_type=f32) + jnp.dot(
            low, ret, preferred_element_type=f32
        )
        out = (x_ref[:, cols].astype(f32) + mixed).astype(bf16)
        out_ref[:, cols] = out
        logits += jnp.sum(out.astype(f32) * head_ref[:, cols], axis=1, keepdims=True)
    coef = loss_scale * (jax.nn.sigmoid(logits) - labels_ref[...].astype(f32))
    coef = jnp.where(is_last, coef, 1.0)
    coef_ref[...] = coef
    picked = jnp.sum(jnp.where(hit0 | hit1, coef, 0.0), axis=0, keepdims=True)
    slots_ref[...] = jnp.where(is_last, picked, 1.0)


def join_backward(
    groups,
    capacity,
    last_ref,
    ret_ref,
    fwd_ref,
    back_ref,
    cot_ref,
    coef_ref,
    gain_ref,
    head_ref,
    fwd_ids_ref,
    back_ids_ref,
    out_ref,
    grad_ref,
    normed_ref,
):
    is_last = last_ref[0] == 1
    ids = jnp.where(is_last, fwd_ids_ref[...], back_ids_ref[...])
    hit0, hit1 = slot_hits(ids, groups, capacity)
    pick = (hit0 | hit1).astype(bf16)
    coef = coef_ref[...]
    x = jnp.where(is_last, fwd_ref[...].astype(f32), back_ref[...].astype(f32))
    inv = inv_rms_of(x)
    dots = jnp.zeros((x.shape[0], 1), f32)
    for cols in chunks(x.shape[1]):
        d_normed = coef * jnp.dot(pick, ret_ref[:, cols], preferred_element_type=f32)
        normed_ref[:, cols] = d_normed
        product = d_normed * x[:, cols]
        dots += jnp.sum(product * gain_ref[:, cols], axis=1, keepdims=True)
        grad_ref[:, cols] = jnp.sum(product * inv, axis=0, keepdims=True)
    scale = inv * inv * inv * (dots / x.shape[1])
    for cols in chunks(x.shape[1]):
        cot = jnp.where(is_last, coef * head_ref[:, cols], cot_ref[:, cols].astype(f32))
        out_ref[:, cols] = (
            cot + inv * (gain_ref[:, cols] * normed_ref[:, cols]) - x[:, cols] * scale
        ).astype(bf16)


def call(kernel, name, outs, args, specs, scratch=()):
    return pl.pallas_call(
        kernel,
        out_shape=[jax.ShapeDtypeStruct(shape, dtype) for shape, dtype in outs],
        in_specs=specs,
        out_specs=[vmem] * len(outs),
        scratch_shapes=list(scratch),
        compiler_params=pltpu.CompilerParams(vmem_limit_bytes=48 << 20),
        name=name,
    )(*args)


def contract_rows(left_op, right_op):
    return lax.dot_general(
        left_op, right_op, (((0,), (0,)), ((), ())), preferred_element_type=f32
    )


def contract_cols(left_op, right_op):
    return lax.dot_general(
        left_op, right_op, (((1,), (1,)), ((), ())), preferred_element_type=f32
    )


def on_device(
    fwd_input,
    back_input,
    cot_input,
    fwd_routes,
    back_routes,
    fwd_gates,
    back_gates,
    w_gate,
    w_up,
    w_down,
    norm_gain,
    verdict_head,
    verdict_labels,
):
    sections = lax.axis_size("section")
    groups = lax.axis_size("expert")
    tok_dev, width = fwd_input.shape[1:]
    top_k = fwd_routes.shape[2]
    capacity = min(tok_dev, 2 * tok_dev * top_k // groups)
    slots = groups * capacity
    x_fwd, x_back, cot = fwd_input[0], back_input[0], cot_input[0]
    wg, wu, wd = w_gate[0, 0], w_up[0, 0], w_down[0, 0]
    head = verdict_head[None]
    last = (lax.axis_index("section") == sections - 1).astype(jnp.int32)[None]

    def bind(kernel):
        def bound(*refs):
            kernel(groups, capacity, *refs)

        return bound

    def exchange(value):
        out = lax.all_to_all(
            value.reshape(groups, capacity, width), "expert", split_axis=0, concat_axis=0, tiled=True
        )
        return out.reshape(slots, width)

    (send_f,) = call(
        bind(send_forward),
        "send_forward",
        [((slots, width), bf16)],
        (x_fwd, norm_gain, fwd_routes[0]),
        [vmem] * 3,
    )
    rows_f = exchange(send_f)
    send_b, send_d = call(
        bind(send_backward),
        "send_backward",
        [((slots, width), bf16)] * 2,
        (
            last,
            x_fwd,
            x_back,
            cot,
            norm_gain,
            head,
            fwd_routes[0],
            back_routes[0],
            fwd_gates[0],
            back_gates[0],
        ),
        [smem] + [vmem] * 9,
    )
    rows_f, send_b, send_d = lax.optimization_barrier((rows_f, send_b, send_d))
    rows_b = exchange(send_b)
    gate_pre = jnp.dot(rows_f, wg, preferred_element_type=f32)
    up_pre = jnp.dot(rows_f, wu, preferred_element_type=f32)
    hidden_f = (jax.nn.silu(gate_pre) * up_pre).astype(bf16)
    out_f = jnp.dot(hidden_f, wd, preferred_element_type=f32).astype(bf16)
    rows_b, send_d = lax.optimization_barrier((rows_b, send_d))
    rows_d = exchange(send_d)
    rows_d, out_f = lax.optimization_barrier((rows_d, out_f))
    ret_f = exchange(out_f)

    gate_pre = jnp.dot(rows_b, wg, preferred_element_type=f32)
    up_pre = jnp.dot(rows_b, wu, preferred_element_type=f32)
    sig = jax.nn.sigmoid(gate_pre)
    silu = gate_pre * sig
    hidden_b = (silu * up_pre).astype(bf16)
    d_hidden = contract_cols(rows_d, wd)
    d_gate = (d_hidden * up_pre * sig * (1.0 + gate_pre * (1.0 - sig))).astype(bf16)
    d_up = (d_hidden * silu).astype(bf16)
    d_rows = (contract_cols(d_gate, wg) + contract_cols(d_up, wu)).astype(bf16)

    ret_f, d_rows = lax.optimization_barrier((ret_f, d_rows))
    ret_d = exchange(d_rows)
    layer_out, coef, coef_slots = call(
        bind(join_forward),
        "join_forward",
        [((tok_dev, width), bf16), ((tok_dev, 1), f32), ((1, slots), f32)],
        (last, ret_f, x_fwd, fwd_routes[0], fwd_gates[0], head, verdict_labels[:, None]),
        [smem] + [vmem] * 6,
    )
    next_input = passed_along(layer_out, "section", 1)
    coef_rows = lax.all_to_all(
        coef_slots.reshape(groups, 1, capacity), "expert", split_axis=0, concat_axis=0, tiled=True
    ).reshape(slots, 1)

    def scaled(value):
        return (value.astype(f32) * coef_rows).astype(bf16)

    grad_d = contract_rows(scaled(hidden_b), rows_d).astype(bf16)
    grad_g = contract_rows(rows_b, scaled(d_gate)).astype(bf16)
    grad_u = contract_rows(rows_b, scaled(d_up)).astype(bf16)

    d_input, gain_local = call(
        bind(join_backward),
        "join_backward",
        [((tok_dev, width), bf16), ((1, width), f32)],
        (last, ret_d, x_fwd, x_back, cot, coef, norm_gain, head, fwd_routes[0], back_routes[0]),
        [smem] + [vmem] * 9,
        [pltpu.VMEM((tok_dev, width), f32)],
    )
    prev_grad = passed_along(d_input, "section", -1)
    shares = lax.all_to_all(
        jnp.broadcast_to(gain_local[None], (groups, 1, width)),
        "expert",
        split_axis=0,
        concat_axis=0,
        tiled=True,
    )
    gain_grad = jnp.sum(shares, axis=0)
    return (
        next_input[None],
        prev_grad[None],
        gain_grad,
        grad_g[None, None],
        grad_u[None, None],
        grad_d[None, None],
    )


def solution(mesh):
    return jax.shard_map(
        on_device,
        mesh=mesh,
        in_specs=(
            P("section", "expert", None),
            P("section", "expert", None),
            P("section", "expert", None),
            P("section", "expert", None),
            P("section", "expert", None),
            P("section", "expert", None),
            P("section", "expert", None),
            P("section", "expert", None, None),
            P("section", "expert", None, None),
            P("section", "expert", None, None),
            P("section", None),
            P(),
            P("expert"),
        ),
        out_specs=(
            P("section", "expert", None),
            P("section", "expert", None),
            P("section", None),
            P("section", "expert", None, None),
            P("section", "expert", None, None),
            P("section", "expert", None, None),
        ),
        check_vma=False,
    )
```

```python
import jax
import jax.numpy as jnp
from jax import lax
from jax.experimental import pallas as pl
from jax.experimental.pallas import tpu as pltpu
from jax.sharding import PartitionSpec as P

loss_scale = 64.0
norm_eps = 1e-06
bf16 = jnp.bfloat16
f32 = jnp.float32
chunk = 512
vmem = pl.BlockSpec(memory_space=pltpu.VMEM)
smem = pl.BlockSpec(memory_space=pltpu.SMEM)


def passed_along(value, axis, steps):
    count = lax.axis_size(axis)
    initial, last = (max(0, -steps), min(count, count - steps))
    return lax.ppermute(value, axis, [(source, source + steps) for source in range(initial, last)])


def slot_keys(ids, groups, capacity):
    tokens = ids.shape[0]
    lanes = lax.broadcasted_iota(jnp.int32, (tokens, 128), 1)
    hit0 = ids[:, 0:1] == lanes
    hit1 = ids[:, 1:2] == lanes
    hits = (hit0 | hit1).astype(bf16)
    before = (
        lax.broadcasted_iota(jnp.int32, (tokens, tokens), 1)
        < lax.broadcasted_iota(jnp.int32, (tokens, tokens), 0)
    ).astype(bf16)
    ranks = jnp.dot(before, hits, preferred_element_type=f32)
    rank0 = jnp.sum(jnp.where(hit0, ranks, 0.0), axis=1, keepdims=True).astype(jnp.int32)
    rank1 = jnp.sum(jnp.where(hit1, ranks, 0.0), axis=1, keepdims=True).astype(jnp.int32)
    return ids[:, 0:1] * capacity + rank0, ids[:, 1:2] * capacity + rank1


def slot_hits(ids, groups, capacity):
    key0, key1 = slot_keys(ids, groups, capacity)
    slots = lax.broadcasted_iota(jnp.int32, (ids.shape[0], groups * capacity), 1)
    return key0 == slots, key1 == slots


def split_weights(hit0, hit1, gates):
    weights = jnp.where(hit0, gates[:, 0:1], 0.0) + jnp.where(hit1, gates[:, 1:2], 0.0)
    high = weights.astype(bf16)
    low = (weights - high.astype(f32)).astype(bf16)
    return high, low


def over_tokens(left, right):
    return lax.dot_general(left, right, (((0,), (0,)), ((), ())), preferred_element_type=f32)


def inv_rms_of(rows):
    return lax.rsqrt(jnp.mean(rows * rows, axis=-1, keepdims=True) + norm_eps)


def chunks(width):
    return [slice(at, min(at + chunk, width)) for at in range(0, width, chunk)]


def send_forward(groups, capacity, x_ref, gain_ref, ids_ref, out_ref):
    hit0, hit1 = slot_hits(ids_ref[...], groups, capacity)
    pick = (hit0 | hit1).astype(bf16)
    x = x_ref[...].astype(f32)
    normed = (x * inv_rms_of(x) * gain_ref[...]).astype(bf16)
    for cols in chunks(x.shape[1]):
        out_ref[:, cols] = over_tokens(pick, normed[:, cols]).astype(bf16)


def send_backward(
    groups,
    capacity,
    last_ref,
    fwd_ref,
    back_ref,
    cot_ref,
    gain_ref,
    head_ref,
    fwd_ids_ref,
    back_ids_ref,
    fwd_gates_ref,
    back_gates_ref,
    out_ref,
):
    is_last = last_ref[0] == 1
    ids = jnp.where(is_last, fwd_ids_ref[...], back_ids_ref[...])
    gates = jnp.where(is_last, fwd_gates_ref[...], back_gates_ref[...])
    hit0, hit1 = slot_hits(ids, groups, capacity)
    pick = (hit0 | hit1).astype(bf16)
    high, low = split_weights(hit0, hit1, gates)
    x = jnp.where(is_last, fwd_ref[...].astype(f32), back_ref[...].astype(f32))
    normed = (x * inv_rms_of(x) * gain_ref[...]).astype(bf16)
    for cols in chunks(x.shape[1]):
        out_ref[:, cols] = over_tokens(pick, normed[:, cols]).astype(bf16)
        cot = cot_ref[:, cols]
        head = jnp.broadcast_to(head_ref[:, cols], cot.shape)
        head_high = head.astype(bf16)
        head_low = (head - head_high.astype(f32)).astype(bf16)
        cot_high = jnp.where(is_last, head_high.astype(f32), cot.astype(f32)).astype(bf16)
        cot_low = jnp.where(is_last, head_low.astype(f32), 0.0).astype(bf16)
        out_ref[:, slice(cols.start + x.shape[1], cols.stop + x.shape[1])] = (
            over_tokens(high, cot_high) + over_tokens(low, cot_high) + over_tokens(high, cot_low)
        ).astype(bf16)


def join_forward(
    groups,
    capacity,
    last_ref,
    ret_ref,
    x_ref,
    ids_ref,
    gates_ref,
    head_ref,
    labels_ref,
    out_ref,
    coef_ref,
    slots_ref,
):
    is_last = last_ref[0] == 1
    hit0, hit1 = slot_hits(ids_ref[...], groups, capacity)
    high, low = split_weights(hit0, hit1, gates_ref[...])
    logits = jnp.zeros((x_ref.shape[0], 1), f32)
    for cols in chunks(x_ref.shape[1]):
        ret = ret_ref[:, cols]
        mixed = jnp.dot(high, ret, preferred_element_type=f32) + jnp.dot(
            low, ret, preferred_element_type=f32
        )
        out = (x_ref[:, cols].astype(f32) + mixed).astype(bf16)
        out_ref[:, cols] = out
        logits += jnp.sum(out.astype(f32) * head_ref[:, cols], axis=1, keepdims=True)
    coef = loss_scale * (jax.nn.sigmoid(logits) - labels_ref[...].astype(f32))
    coef = jnp.where(is_last, coef, 1.0)
    coef_ref[...] = coef
    picked = jnp.sum(jnp.where(hit0 | hit1, coef, 0.0), axis=0, keepdims=True)
    slots_ref[...] = jnp.where(is_last, picked, 1.0)


def join_backward(
    groups,
    capacity,
    last_ref,
    ret_ref,
    fwd_ref,
    back_ref,
    cot_ref,
    coef_ref,
    gain_ref,
    head_ref,
    fwd_ids_ref,
    back_ids_ref,
    out_ref,
    grad_ref,
    normed_ref,
):
    is_last = last_ref[0] == 1
    ids = jnp.where(is_last, fwd_ids_ref[...], back_ids_ref[...])
    hit0, hit1 = slot_hits(ids, groups, capacity)
    pick = (hit0 | hit1).astype(bf16)
    coef = coef_ref[...]
    x = jnp.where(is_last, fwd_ref[...].astype(f32), back_ref[...].astype(f32))
    inv = inv_rms_of(x)
    dots = jnp.zeros((x.shape[0], 1), f32)
    for cols in chunks(x.shape[1]):
        d_normed = coef * jnp.dot(pick, ret_ref[:, cols], preferred_element_type=f32)
        normed_ref[:, cols] = d_normed
        product = d_normed * x[:, cols]
        dots += jnp.sum(product * gain_ref[:, cols], axis=1, keepdims=True)
        grad_ref[:, cols] = jnp.sum(product * inv, axis=0, keepdims=True)
    scale = inv * inv * inv * (dots / x.shape[1])
    for cols in chunks(x.shape[1]):
        cot = jnp.where(is_last, coef * head_ref[:, cols], cot_ref[:, cols].astype(f32))
        out_ref[:, cols] = (
            cot + inv * (gain_ref[:, cols] * normed_ref[:, cols]) - x[:, cols] * scale
        ).astype(bf16)


def call(kernel, name, outs, args, specs, scratch=()):
    return pl.pallas_call(
        kernel,
        out_shape=[jax.ShapeDtypeStruct(shape, dtype) for shape, dtype in outs],
        in_specs=specs,
        out_specs=[vmem] * len(outs),
        scratch_shapes=list(scratch),
        compiler_params=pltpu.CompilerParams(vmem_limit_bytes=48 << 20),
        name=name,
    )(*args)


def contract_rows(left_op, right_op):
    return lax.dot_general(
        left_op, right_op, (((0,), (0,)), ((), ())), preferred_element_type=f32
    )


def contract_cols(left_op, right_op):
    return lax.dot_general(
        left_op, right_op, (((1,), (1,)), ((), ())), preferred_element_type=f32
    )


def on_device(
    fwd_input,
    back_input,
    cot_input,
    fwd_routes,
    back_routes,
    fwd_gates,
    back_gates,
    w_gate,
    w_up,
    w_down,
    norm_gain,
    verdict_head,
    verdict_labels,
):
    sections = lax.axis_size("section")
    groups = lax.axis_size("expert")
    tok_dev, width = fwd_input.shape[1:]
    top_k = fwd_routes.shape[2]
    capacity = min(tok_dev, 2 * tok_dev * top_k // groups)
    slots = groups * capacity
    x_fwd, x_back, cot = fwd_input[0], back_input[0], cot_input[0]
    wg, wu, wd = w_gate[0, 0], w_up[0, 0], w_down[0, 0]
    head = verdict_head[None]
    last = (lax.axis_index("section") == sections - 1).astype(jnp.int32)[None]

    def bind(kernel):
        def bound(*refs):
            kernel(groups, capacity, *refs)

        return bound

    def exchange(value):
        out = lax.all_to_all(
            value.reshape(groups, capacity, value.shape[1]),
            "expert",
            split_axis=0,
            concat_axis=0,
            tiled=True,
        )
        return out.reshape(value.shape)

    (send_f,) = call(
        bind(send_forward),
        "send_forward",
        [((slots, width), bf16)],
        (x_fwd, norm_gain, fwd_routes[0]),
        [vmem] * 3,
    )
    rows_f = exchange(send_f)
    (send_b,) = call(
        bind(send_backward),
        "send_backward",
        [((slots, 2 * width), bf16)],
        (
            last,
            x_fwd,
            x_back,
            cot,
            norm_gain,
            head,
            fwd_routes[0],
            back_routes[0],
            fwd_gates[0],
            back_gates[0],
        ),
        [smem] + [vmem] * 9,
    )
    rows_f, send_b = lax.optimization_barrier((rows_f, send_b))
    rows_bd = exchange(send_b)
    gate_pre = jnp.dot(rows_f, wg, preferred_element_type=f32)
    up_pre = jnp.dot(rows_f, wu, preferred_element_type=f32)
    hidden_f = (jax.nn.silu(gate_pre) * up_pre).astype(bf16)
    out_f = jnp.dot(hidden_f, wd, preferred_element_type=f32).astype(bf16)
    rows_bd, out_f = lax.optimization_barrier((rows_bd, out_f))
    ret_f = exchange(out_f)

    rows_b, rows_d = rows_bd[:, :width], rows_bd[:, width:]
    gate_pre = jnp.dot(rows_b, wg, preferred_element_type=f32)
    up_pre = jnp.dot(rows_b, wu, preferred_element_type=f32)
    sig = jax.nn.sigmoid(gate_pre)
    silu = gate_pre * sig
    hidden_b = (silu * up_pre).astype(bf16)
    d_hidden = contract_cols(rows_d, wd)
    d_gate = (d_hidden * up_pre * sig * (1.0 + gate_pre * (1.0 - sig))).astype(bf16)
    d_up = (d_hidden * silu).astype(bf16)
    d_rows = (contract_cols(d_gate, wg) + contract_cols(d_up, wu)).astype(bf16)

    ret_f, d_rows = lax.optimization_barrier((ret_f, d_rows))
    ret_d = exchange(d_rows)
    layer_out, coef, coef_slots = call(
        bind(join_forward),
        "join_forward",
        [((tok_dev, width), bf16), ((tok_dev, 1), f32), ((1, slots), f32)],
        (last, ret_f, x_fwd, fwd_routes[0], fwd_gates[0], head, verdict_labels[:, None]),
        [smem] + [vmem] * 6,
    )
    mine = lax.axis_index("expert")
    table = jnp.where(jnp.arange(groups)[:, None] == mine, coef_slots, 0.0)
    step = 1
    while step < groups:
        table = table + lax.ppermute(
            table, "expert", [(source, source ^ step) for source in range(groups)]
        )
        step *= 2
    next_input = passed_along(layer_out, "section", 1)
    coef_rows = lax.dynamic_slice_in_dim(table, mine * capacity, capacity, axis=1).reshape(slots, 1)

    def scaled(value):
        return (value.astype(f32) * coef_rows).astype(bf16)

    grad_d = contract_rows(scaled(hidden_b), rows_d).astype(bf16)
    grad_g = contract_rows(rows_b, scaled(d_gate)).astype(bf16)
    grad_u = contract_rows(rows_b, scaled(d_up)).astype(bf16)

    ret_d, next_input, grad_d, grad_g, grad_u = lax.optimization_barrier(
        (ret_d, next_input, grad_d, grad_g, grad_u)
    )
    d_input, gain_local = call(
        bind(join_backward),
        "join_backward",
        [((tok_dev, width), bf16), ((1, width), f32)],
        (last, ret_d, x_fwd, x_back, cot, coef, norm_gain, head, fwd_routes[0], back_routes[0]),
        [smem] + [vmem] * 9,
        [pltpu.VMEM((tok_dev, width), f32)],
    )
    prev_grad = passed_along(d_input, "section", -1)
    shares = lax.all_to_all(
        jnp.broadcast_to(gain_local[None], (groups, 1, width)),
        "expert",
        split_axis=0,
        concat_axis=0,
        tiled=True,
    )
    gain_grad = jnp.sum(shares, axis=0)
    return (
        next_input[None],
        prev_grad[None],
        gain_grad,
        grad_g[None, None],
        grad_u[None, None],
        grad_d[None, None],
    )


def solution(mesh):
    return jax.shard_map(
        on_device,
        mesh=mesh,
        in_specs=(
            P("section", "expert", None),
            P("section", "expert", None),
            P("section", "expert", None),
            P("section", "expert", None),
            P("section", "expert", None),
            P("section", "expert", None),
            P("section", "expert", None),
            P("section", "expert", None, None),
            P("section", "expert", None, None),
            P("section", "expert", None, None),
            P("section", None),
            P(),
            P("expert"),
        ),
        out_specs=(
            P("section", "expert", None),
            P("section", "expert", None),
            P("section", None),
            P("section", "expert", None, None),
            P("section", "expert", None, None),
            P("section", "expert", None, None),
        ),
        check_vma=False,
    )
```

```python
import jax
import jax.numpy as jnp
from jax import lax
from jax.experimental import pallas as pl
from jax.experimental.pallas import tpu as pltpu
from jax.sharding import PartitionSpec as P

loss_scale = 64.0
norm_eps = 1e-06
bf16 = jnp.bfloat16
f32 = jnp.float32
chunk = 512
extra = 128
vmem = pl.BlockSpec(memory_space=pltpu.VMEM)
smem = pl.BlockSpec(memory_space=pltpu.SMEM)


def passed_along(value, axis, steps):
    count = lax.axis_size(axis)
    initial, last = (max(0, -steps), min(count, count - steps))
    return lax.ppermute(value, axis, [(source, source + steps) for source in range(initial, last)])


def slot_keys(ids, groups, capacity):
    tokens = ids.shape[0]
    lanes = lax.broadcasted_iota(jnp.int32, (tokens, 128), 1)
    hit0 = ids[:, 0:1] == lanes
    hit1 = ids[:, 1:2] == lanes
    hits = (hit0 | hit1).astype(bf16)
    before = (
        lax.broadcasted_iota(jnp.int32, (tokens, tokens), 1)
        < lax.broadcasted_iota(jnp.int32, (tokens, tokens), 0)
    ).astype(bf16)
    ranks = jnp.dot(before, hits, preferred_element_type=f32)
    rank0 = jnp.sum(jnp.where(hit0, ranks, 0.0), axis=1, keepdims=True).astype(jnp.int32)
    rank1 = jnp.sum(jnp.where(hit1, ranks, 0.0), axis=1, keepdims=True).astype(jnp.int32)
    return ids[:, 0:1] * capacity + rank0, ids[:, 1:2] * capacity + rank1


def slot_hits(ids, groups, capacity):
    key0, key1 = slot_keys(ids, groups, capacity)
    slots = lax.broadcasted_iota(jnp.int32, (ids.shape[0], groups * capacity), 1)
    return key0 == slots, key1 == slots


def split_weights(hit0, hit1, gates):
    weights = jnp.where(hit0, gates[:, 0:1], 0.0) + jnp.where(hit1, gates[:, 1:2], 0.0)
    high = weights.astype(bf16)
    low = (weights - high.astype(f32)).astype(bf16)
    return high, low


def over_tokens(left, right):
    return lax.dot_general(left, right, (((0,), (0,)), ((), ())), preferred_element_type=f32)


def inv_rms_of(rows):
    return lax.rsqrt(jnp.mean(rows * rows, axis=-1, keepdims=True) + norm_eps)


def chunks(width):
    return [slice(at, min(at + chunk, width)) for at in range(0, width, chunk)]


def send_forward(groups, capacity, x_ref, gain_ref, ids_ref, out_ref):
    hit0, hit1 = slot_hits(ids_ref[...], groups, capacity)
    pick = (hit0 | hit1).astype(bf16)
    x = x_ref[...].astype(f32)
    normed = (x * inv_rms_of(x) * gain_ref[...]).astype(bf16)
    for cols in chunks(x.shape[1]):
        out_ref[:, cols] = over_tokens(pick, normed[:, cols]).astype(bf16)


def send_backward(
    groups,
    capacity,
    last_ref,
    fwd_ref,
    back_ref,
    cot_ref,
    gain_ref,
    head_ref,
    fwd_ids_ref,
    back_ids_ref,
    fwd_gates_ref,
    back_gates_ref,
    rows_ref,
    dout_ref,
    x_ref,
):
    is_last = last_ref[0] == 1
    ids = jnp.where(is_last, fwd_ids_ref[...], back_ids_ref[...])
    gates = jnp.where(is_last, fwd_gates_ref[...], back_gates_ref[...])
    hit0, hit1 = slot_hits(ids, groups, capacity)
    pick = (hit0 | hit1).astype(bf16)
    high, low = split_weights(hit0, hit1, gates)
    x = jnp.where(is_last, fwd_ref[...].astype(f32), back_ref[...].astype(f32))
    x_ref[...] = x.astype(bf16)
    normed = (x * inv_rms_of(x) * gain_ref[...]).astype(bf16)
    dout_ref[:, x.shape[1] :] = jnp.zeros((dout_ref.shape[0], extra), bf16)
    for cols in chunks(x.shape[1]):
        rows_ref[:, cols] = over_tokens(pick, normed[:, cols]).astype(bf16)
        cot = cot_ref[:, cols]
        head = jnp.broadcast_to(head_ref[:, cols], cot.shape)
        head_high = head.astype(bf16)
        head_low = (head - head_high.astype(f32)).astype(bf16)
        cot_high = jnp.where(is_last, head_high.astype(f32), cot.astype(f32)).astype(bf16)
        cot_low = jnp.where(is_last, head_low.astype(f32), 0.0).astype(bf16)
        dout_ref[:, cols] = (
            over_tokens(high, cot_high) + over_tokens(low, cot_high) + over_tokens(high, cot_low)
        ).astype(bf16)


def in_parts(column):
    lanes = lax.broadcasted_iota(jnp.int32, (column.shape[0], extra), 1)
    out = jnp.zeros((column.shape[0], extra), f32)
    rest = column
    for lane in range(3):
        part = rest.astype(bf16).astype(f32)
        out = jnp.where(lanes == lane, part, out)
        rest = rest - part
    return out.astype(bf16)


def attach_dots(out_ref, head_ref, unused_ref, block_ref, ret_ref):
    width = out_ref.shape[1]
    dots = jnp.zeros((out_ref.shape[0], 1), f32)
    for cols in chunks(width):
        out = out_ref[:, cols]
        ret_ref[:, cols] = out
        dots += jnp.sum(out.astype(f32) * head_ref[:, cols], axis=1, keepdims=True)
    ret_ref[:, width:] = jnp.zeros((out_ref.shape[0], extra), bf16)
    block_ref[...] = in_parts(dots)


def find_coefs(
    groups,
    capacity,
    last_ref,
    x_ref,
    ids_ref,
    gates_ref,
    head_ref,
    labels_ref,
    dots_ref,
    unused_ref,
    coef_ref,
    block_ref,
):
    is_last = last_ref[0] == 1
    hit0, hit1 = slot_hits(ids_ref[...], groups, capacity)
    high, low = split_weights(hit0, hit1, gates_ref[...])
    pick = (hit0 | hit1).astype(bf16)
    dots = dots_ref[...]
    mixed = jnp.dot(high, dots, preferred_element_type=f32) + jnp.dot(
        low, dots, preferred_element_type=f32
    )
    logits = jnp.sum(mixed, axis=1, keepdims=True)
    logits += jnp.sum(x_ref[...].astype(f32) * head_ref[...], axis=1, keepdims=True)
    coef = loss_scale * (jax.nn.sigmoid(logits) - labels_ref[...].astype(f32))
    coef = jnp.where(is_last, coef, 1.0)
    coef_ref[...] = coef
    picked = over_tokens(pick, in_parts(coef))
    ones = (lax.broadcasted_iota(jnp.int32, picked.shape, 1) == 0).astype(f32)
    block_ref[...] = jnp.where(is_last, picked, ones).astype(bf16)


def join_forward(groups, capacity, ret_ref, x_ref, ids_ref, gates_ref, out_ref):
    hit0, hit1 = slot_hits(ids_ref[...], groups, capacity)
    high, low = split_weights(hit0, hit1, gates_ref[...])
    for cols in chunks(x_ref.shape[1]):
        ret = ret_ref[:, cols]
        mixed = jnp.dot(high, ret, preferred_element_type=f32) + jnp.dot(
            low, ret, preferred_element_type=f32
        )
        out_ref[:, cols] = (x_ref[:, cols].astype(f32) + mixed).astype(bf16)


def copy_rows(in_ref, out_ref):
    out_ref[...] = in_ref[...]


def join_backward(
    groups,
    capacity,
    last_ref,
    ret_ref,
    x_ref,
    cot_ref,
    coef_ref,
    gain_ref,
    head_ref,
    fwd_ids_ref,
    back_ids_ref,
    out_ref,
    grad_ref,
    normed_ref,
):
    is_last = last_ref[0] == 1
    ids = jnp.where(is_last, fwd_ids_ref[...], back_ids_ref[...])
    hit0, hit1 = slot_hits(ids, groups, capacity)
    pick = (hit0 | hit1).astype(bf16)
    coef = coef_ref[...]
    x = x_ref[...].astype(f32)
    inv = inv_rms_of(x)
    dots = jnp.zeros((x.shape[0], 1), f32)
    for cols in chunks(x.shape[1]):
        d_normed = coef * jnp.dot(pick, ret_ref[:, cols], preferred_element_type=f32)
        normed_ref[:, cols] = d_normed
        product = d_normed * x[:, cols]
        dots += jnp.sum(product * gain_ref[:, cols], axis=1, keepdims=True)
        grad_ref[:, cols] = jnp.sum(product * inv, axis=0, keepdims=True)
    scale = inv * inv * inv * (dots / x.shape[1])
    for cols in chunks(x.shape[1]):
        cot = jnp.where(is_last, coef * head_ref[:, cols], cot_ref[:, cols].astype(f32))
        out_ref[:, cols] = (
            cot + inv * (gain_ref[:, cols] * normed_ref[:, cols]) - x[:, cols] * scale
        ).astype(bf16)


def call(kernel, name, outs, args, specs, scratch=(), out_specs=None, aliases=None):
    return pl.pallas_call(
        kernel,
        out_shape=[jax.ShapeDtypeStruct(shape, dtype) for shape, dtype in outs],
        grid=(1,),
        in_specs=specs,
        out_specs=out_specs or [vmem] * len(outs),
        scratch_shapes=list(scratch),
        input_output_aliases=aliases or {},
        compiler_params=pltpu.CompilerParams(vmem_limit_bytes=48 << 20),
        name=name,
    )(*args)


def contract_rows(left_op, right_op):
    return lax.dot_general(
        left_op, right_op, (((0,), (0,)), ((), ())), preferred_element_type=f32
    )


def contract_cols(left_op, right_op):
    return lax.dot_general(
        left_op, right_op, (((1,), (1,)), ((), ())), preferred_element_type=f32
    )


def on_device(
    fwd_input,
    back_input,
    cot_input,
    fwd_routes,
    back_routes,
    fwd_gates,
    back_gates,
    w_gate,
    w_up,
    w_down,
    norm_gain,
    verdict_head,
    verdict_labels,
):
    sections = lax.axis_size("section")
    groups = lax.axis_size("expert")
    tok_dev, width = fwd_input.shape[1:]
    top_k = fwd_routes.shape[2]
    capacity = min(tok_dev, 2 * tok_dev * top_k // groups)
    slots = groups * capacity
    x_fwd, x_back, cot = fwd_input[0], back_input[0], cot_input[0]
    wg, wu, wd = w_gate[0, 0], w_up[0, 0], w_down[0, 0]
    head = verdict_head[None]
    last = (lax.axis_index("section") == sections - 1).astype(jnp.int32)[None]

    def bind(kernel):
        def bound(*refs):
            kernel(groups, capacity, *refs)

        return bound

    def exchange(value):
        out = lax.all_to_all(
            value.reshape(groups, capacity, value.shape[1]),
            "expert",
            split_axis=0,
            concat_axis=0,
            tiled=True,
        )
        return out.reshape(value.shape)

    (send_f,) = call(
        bind(send_forward),
        "send_forward",
        [((slots, width), bf16)],
        (x_fwd, norm_gain, fwd_routes[0]),
        [vmem] * 3,
    )
    rows_f = exchange(send_f)
    last_block = pl.BlockSpec((slots, extra), lambda i: (0, width // extra))
    send_b, send_d, x_sel = call(
        bind(send_backward),
        "send_backward",
        [((slots, width), bf16), ((slots, width + extra), bf16), ((tok_dev, width), bf16)],
        (
            last,
            x_fwd,
            x_back,
            cot,
            norm_gain,
            head,
            fwd_routes[0],
            back_routes[0],
            fwd_gates[0],
            back_gates[0],
        ),
        [smem] + [vmem] * 9,
    )
    rows_f, send_b = lax.optimization_barrier((rows_f, send_b))
    rows_b = exchange(send_b)
    gate_pre = jnp.dot(rows_f, wg, preferred_element_type=f32)
    up_pre = jnp.dot(rows_f, wu, preferred_element_type=f32)
    hidden_f = (jax.nn.silu(gate_pre) * up_pre).astype(bf16)
    out_f = jnp.dot(hidden_f, wd, preferred_element_type=f32).astype(bf16)
    send_d, ret_send = call(
        attach_dots,
        "attach_dots",
        [((slots, width + extra), bf16)] * 2,
        (out_f, head, send_d),
        [vmem, vmem, last_block],
        out_specs=[last_block, vmem],
        aliases={2: 0},
    )
    rows_b, send_d = lax.optimization_barrier((rows_b, send_d))
    rows_d = exchange(send_d)
    coef, ret_send = call(
        bind(find_coefs),
        "find_coefs",
        [((tok_dev, 1), f32), ((slots, width + extra), bf16)],
        (
            last,
            x_fwd,
            fwd_routes[0],
            fwd_gates[0],
            head,
            verdict_labels[:, None],
            rows_d,
            ret_send,
        ),
        [smem] + [vmem] * 5 + [last_block] * 2,
        out_specs=[vmem, last_block],
        aliases={7: 1},
    )
    ret_f = exchange(ret_send)

    gate_pre = jnp.dot(rows_b, wg, preferred_element_type=f32)
    up_pre = jnp.dot(rows_b, wu, preferred_element_type=f32)
    sig = jax.nn.sigmoid(gate_pre)
    silu = gate_pre * sig
    hidden_b = (silu * up_pre).astype(bf16)
    rows_d = rows_d[:, :width]
    d_hidden = contract_cols(rows_d, wd)
    d_gate = (d_hidden * up_pre * sig * (1.0 + gate_pre * (1.0 - sig))).astype(bf16)
    d_up = (d_hidden * silu).astype(bf16)
    d_rows = (contract_cols(d_gate, wg) + contract_cols(d_up, wu)).astype(bf16)

    ret_f, d_rows = lax.optimization_barrier((ret_f, d_rows))
    ret_d = exchange(d_rows)
    (layer_out,) = call(
        bind(join_forward),
        "join_forward",
        [((tok_dev, width), bf16)],
        (ret_f, x_fwd, fwd_routes[0], fwd_gates[0]),
        [vmem] * 4,
    )
    next_input = passed_along(layer_out, "section", 1)
    (next_input,) = call(
        copy_rows, "copy_rows", [((tok_dev, width), bf16)], (next_input,), [vmem]
    )
    coef_rows = jnp.sum(ret_f[:, width:].astype(f32), axis=1, keepdims=True)

    def scaled(value):
        return (value.astype(f32) * coef_rows).astype(bf16)

    grad_d = contract_rows(scaled(hidden_b), rows_d).astype(bf16)
    grad_g = contract_rows(rows_b, scaled(d_gate)).astype(bf16)
    grad_u = contract_rows(rows_b, scaled(d_up)).astype(bf16)

    ret_d, next_input, grad_d, grad_g, grad_u = lax.optimization_barrier(
        (ret_d, next_input, grad_d, grad_g, grad_u)
    )
    d_input, gain_local = call(
        bind(join_backward),
        "join_backward",
        [((tok_dev, width), bf16), ((1, width), f32)],
        (last, ret_d, x_sel, cot, coef, norm_gain, head, fwd_routes[0], back_routes[0]),
        [smem] + [vmem] * 8,
        [pltpu.VMEM((tok_dev, width), f32)],
    )
    prev_grad = passed_along(d_input, "section", -1)
    shares = lax.all_to_all(
        jnp.broadcast_to(gain_local[None], (groups, 1, width)),
        "expert",
        split_axis=0,
        concat_axis=0,
        tiled=True,
    )
    gain_grad = jnp.sum(shares, axis=0)
    return (
        next_input[None],
        prev_grad[None],
        gain_grad,
        grad_g[None, None],
        grad_u[None, None],
        grad_d[None, None],
    )


def solution(mesh):
    return jax.shard_map(
        on_device,
        mesh=mesh,
        in_specs=(
            P("section", "expert", None),
            P("section", "expert", None),
            P("section", "expert", None),
            P("section", "expert", None),
            P("section", "expert", None),
            P("section", "expert", None),
            P("section", "expert", None),
            P("section", "expert", None, None),
            P("section", "expert", None, None),
            P("section", "expert", None, None),
            P("section", None),
            P(),
            P("expert"),
        ),
        out_specs=(
            P("section", "expert", None),
            P("section", "expert", None),
            P("section", None),
            P("section", "expert", None, None),
            P("section", "expert", None, None),
            P("section", "expert", None, None),
        ),
        check_vma=False,
    )
```

```python
import jax
import jax.numpy as jnp
from jax import lax
from jax.experimental import pallas as pl
from jax.experimental.pallas import tpu as pltpu
from jax.sharding import PartitionSpec as P

loss_scale = 64.0
norm_eps = 1e-06
bf16 = jnp.bfloat16
f32 = jnp.float32
chunk = 512
extra = 128
steps = (0, -1, 1, 2)
vmem = pl.BlockSpec(memory_space=pltpu.VMEM)
smem = pl.BlockSpec(memory_space=pltpu.SMEM)


def passed_along(value, axis, steps):
    count = lax.axis_size(axis)
    initial, last = (max(0, -steps), min(count, count - steps))
    return lax.ppermute(value, axis, [(source, source + steps) for source in range(initial, last)])


def slot_keys(ids, groups, capacity):
    tokens = ids.shape[0]
    lanes = lax.broadcasted_iota(jnp.int32, (tokens, 128), 1)
    hit0 = ids[:, 0:1] == lanes
    hit1 = ids[:, 1:2] == lanes
    hits = (hit0 | hit1).astype(bf16)
    before = (
        lax.broadcasted_iota(jnp.int32, (tokens, tokens), 1)
        < lax.broadcasted_iota(jnp.int32, (tokens, tokens), 0)
    ).astype(bf16)
    ranks = jnp.dot(before, hits, preferred_element_type=f32)
    rank0 = jnp.sum(jnp.where(hit0, ranks, 0.0), axis=1, keepdims=True).astype(jnp.int32)
    rank1 = jnp.sum(jnp.where(hit1, ranks, 0.0), axis=1, keepdims=True).astype(jnp.int32)
    return ids[:, 0:1] * capacity + rank0, ids[:, 1:2] * capacity + rank1


def slot_hits(ids, groups, capacity):
    key0, key1 = slot_keys(ids, groups, capacity)
    slots = lax.broadcasted_iota(jnp.int32, (ids.shape[0], groups * capacity), 1)
    return key0 == slots, key1 == slots


def split_weights(hit0, hit1, gates):
    weights = jnp.where(hit0, gates[:, 0:1], 0.0) + jnp.where(hit1, gates[:, 1:2], 0.0)
    high = weights.astype(bf16)
    low = (weights - high.astype(f32)).astype(bf16)
    return high, low


def over_tokens(left, right):
    return lax.dot_general(left, right, (((0,), (0,)), ((), ())), preferred_element_type=f32)


def inv_rms_of(rows):
    return lax.rsqrt(jnp.mean(rows * rows, axis=-1, keepdims=True) + norm_eps)


def chunks(width):
    return [slice(at, min(at + chunk, width)) for at in range(0, width, chunk)]


def ranked(hit):
    tokens = hit.shape[0]
    before = (
        lax.broadcasted_iota(jnp.int32, (tokens, tokens), 1)
        < lax.broadcasted_iota(jnp.int32, (tokens, tokens), 0)
    ).astype(bf16)
    return jnp.dot(before, hit.astype(bf16), preferred_element_type=f32).astype(jnp.int32)


def pick_rows(
    groups,
    capacity,
    place_ref,
    own_ref,
    below_ref,
    above_ref,
    far_low_ref,
    far_high_ref,
    gain_ref,
    ids_ref,
    near_ref,
    other_ref,
):
    mine = place_ref[1]
    far = jnp.concatenate([far_low_ref[...], far_high_ref[...]], axis=0)
    tokens, width = own_ref.shape
    lanes = lax.broadcasted_iota(jnp.int32, (tokens, 2 * capacity), 1)
    wanted = jnp.where(lanes < capacity, mine, mine ^ 1)
    for at, rows in enumerate((own_ref[...], below_ref[...], above_ref[...], far)):
        ids = ids_ref[at]
        hit = (ids[:, 0:1] == wanted) | (ids[:, 1:2] == wanted)
        pick = (hit & (ranked(hit) == (lanes & (capacity - 1)))).astype(bf16)
        x = rows.astype(f32)
        normed = (x * inv_rms_of(x) * gain_ref[...]).astype(bf16)
        place = slice(at * capacity, (at + 1) * capacity)
        for cols in chunks(width):
            got = over_tokens(pick, normed[:, cols]).astype(bf16)
            near_ref[place, cols] = got[:capacity]
            other_ref[place, cols] = got[capacity:]


def weigh_rows(
    groups, capacity, place_ref, own_ref, pair_ref, head_ref, ids_ref, gates_ref, *out_refs
):
    is_last = place_ref[0] == 1
    mine = place_ref[1]
    tokens, width = own_ref.shape
    lanes = lax.broadcasted_iota(jnp.int32, (tokens, len(out_refs) * capacity), 1)
    wanted = (mine + 2 * lax.div(lanes, capacity)) & (groups - 1)
    for side, cot_ref in enumerate((own_ref, pair_ref)):
        ids = ids_ref[side]
        hit0, hit1 = ids[:, 0:1] == wanted, ids[:, 1:2] == wanted
        inside = ranked(hit0 | hit1) == (lanes & (capacity - 1))
        high, low = split_weights(hit0 & inside, hit1 & inside, gates_ref[side])
        for cols in chunks(width):
            cot = cot_ref[:, cols]
            head = jnp.broadcast_to(head_ref[:, cols], cot.shape)
            head_high = head.astype(bf16)
            head_low = (head - head_high.astype(f32)).astype(bf16)
            cot_high = jnp.where(is_last, head_high.astype(f32), cot.astype(f32)).astype(bf16)
            cot_low = jnp.where(is_last, head_low.astype(f32), 0.0).astype(bf16)
            dout = (
                over_tokens(high, cot_high) + over_tokens(low, cot_high) + over_tokens(high, cot_low)
            ).astype(bf16)
            for at, ref in enumerate(out_refs):
                ref[side * capacity : (side + 1) * capacity, cols] = dout[
                    at * capacity : (at + 1) * capacity
                ]


def in_parts(column):
    lanes = lax.broadcasted_iota(jnp.int32, (column.shape[0], extra), 1)
    out = jnp.zeros((column.shape[0], extra), f32)
    rest = column
    for lane in range(3):
        part = rest.astype(bf16).astype(f32)
        out = jnp.where(lanes == lane, part, out)
        rest = rest - part
    return out.astype(bf16)


def sources(mine):
    return [((mine + 2 * (step + 4)) & 7) ^ side for side in (0, 1) for step in steps]


def attach_dots(groups, capacity, place_ref, out_ref, head_ref, ret_ref, dots_ref):
    width = out_ref.shape[1]
    rows = lax.broadcasted_iota(jnp.int32, (8, width), 0)
    parts = jnp.zeros((8, width), f32)
    rest = head_ref[...]
    for row in range(3):
        part = rest.astype(bf16).astype(f32)
        parts = jnp.where(rows == row, part, parts)
        rest = rest - part
    parts = parts.astype(bf16)
    for at, source in enumerate(sources(place_ref[1])):
        out = out_ref[at * capacity : (at + 1) * capacity, :]
        ret_ref[source, :, :width] = out
        ret_ref[source, :, width:] = jnp.zeros((capacity, extra), bf16)
        dots = lax.dot_general(parts, out, (((1,), (1,)), ((), ())), preferred_element_type=f32)
        dots_ref[source] = jnp.sum(dots, axis=0, keepdims=True)


def split_rows(groups, capacity, place_ref, in_ref, out_ref):
    for at, source in enumerate(sources(place_ref[1])):
        out_ref[source] = in_ref[at * capacity : (at + 1) * capacity, :]


def find_coefs(
    groups,
    capacity,
    place_ref,
    x_ref,
    ids_ref,
    gates_ref,
    head_ref,
    labels_ref,
    dots_ref,
    unused_ref,
    coef_ref,
    block_ref,
):
    is_last = place_ref[0] == 1
    hit0, hit1 = slot_hits(ids_ref[...], groups, capacity)
    gates = gates_ref[...]
    pick = (hit0 | hit1).astype(bf16)
    weights = jnp.where(hit0, gates[:, 0:1], 0.0) + jnp.where(hit1, gates[:, 1:2], 0.0)
    logits = jnp.zeros((x_ref.shape[0], 1), f32)
    for at in range(groups):
        block = weights[:, at * capacity : (at + 1) * capacity]
        logits += jnp.sum(block * dots_ref[at], axis=1, keepdims=True)
    logits += jnp.sum(x_ref[...].astype(f32) * head_ref[...], axis=1, keepdims=True)
    coef = loss_scale * (jax.nn.sigmoid(logits) - labels_ref[...].astype(f32))
    coef = jnp.where(is_last, coef, 1.0)
    coef_ref[...] = coef
    picked = over_tokens(pick, in_parts(coef))
    ones = (lax.broadcasted_iota(jnp.int32, picked.shape, 1) == 0).astype(f32)
    block_ref[...] = jnp.where(is_last, picked, ones).astype(bf16)


def join_forward(groups, capacity, ret_ref, x_ref, ids_ref, gates_ref, out_ref):
    hit0, hit1 = slot_hits(ids_ref[...], groups, capacity)
    high, low = split_weights(hit0, hit1, gates_ref[...])
    for cols in chunks(x_ref.shape[1]):
        ret = ret_ref[:, cols]
        mixed = jnp.dot(high, ret, preferred_element_type=f32) + jnp.dot(
            low, ret, preferred_element_type=f32
        )
        out_ref[:, cols] = (x_ref[:, cols].astype(f32) + mixed).astype(bf16)


def copy_rows(in_ref, unused_ref, out_ref):
    out_ref[...] = in_ref[...]


def join_backward(
    groups,
    capacity,
    place_ref,
    ret_ref,
    x_ref,
    cot_ref,
    coef_ref,
    gain_ref,
    head_ref,
    fwd_ids_ref,
    back_ids_ref,
    out_ref,
    grad_ref,
    normed_ref,
):
    is_last = place_ref[0] == 1
    ids = jnp.where(is_last, fwd_ids_ref[...], back_ids_ref[...])
    hit0, hit1 = slot_hits(ids, groups, capacity)
    pick = (hit0 | hit1).astype(bf16)
    coef = coef_ref[...]
    x = x_ref[...].astype(f32)
    inv = inv_rms_of(x)
    dots = jnp.zeros((x.shape[0], 1), f32)
    for cols in chunks(x.shape[1]):
        d_normed = coef * jnp.dot(pick, ret_ref[:, cols], preferred_element_type=f32)
        normed_ref[:, cols] = d_normed
        product = d_normed * x[:, cols]
        dots += jnp.sum(product * gain_ref[:, cols], axis=1, keepdims=True)
        grad_ref[:, cols] = jnp.sum(product * inv, axis=0, keepdims=True)
    scale = inv * inv * inv * (dots / x.shape[1])
    for cols in chunks(x.shape[1]):
        cot = jnp.where(is_last, coef * head_ref[:, cols], cot_ref[:, cols].astype(f32))
        out_ref[:, cols] = (
            cot + inv * (gain_ref[:, cols] * normed_ref[:, cols]) - x[:, cols] * scale
        ).astype(bf16)


def call(kernel, name, outs, args, specs, scratch=(), out_specs=None, aliases=None):
    return pl.pallas_call(
        kernel,
        out_shape=[jax.ShapeDtypeStruct(shape, dtype) for shape, dtype in outs],
        grid=(1,),
        in_specs=specs,
        out_specs=out_specs or [vmem] * len(outs),
        scratch_shapes=list(scratch),
        input_output_aliases=aliases or {},
        compiler_params=pltpu.CompilerParams(vmem_limit_bytes=48 << 20),
        name=name,
    )(*args)


def contract_rows(left_op, right_op):
    return lax.dot_general(
        left_op, right_op, (((0,), (0,)), ((), ())), preferred_element_type=f32
    )


def contract_cols(left_op, right_op):
    return lax.dot_general(
        left_op, right_op, (((1,), (1,)), ((), ())), preferred_element_type=f32
    )


def on_device(
    fwd_input,
    back_input,
    cot_input,
    fwd_routes,
    back_routes,
    fwd_gates,
    back_gates,
    w_gate,
    w_up,
    w_down,
    norm_gain,
    verdict_head,
    verdict_labels,
):
    sections = lax.axis_size("section")
    groups = lax.axis_size("expert")
    tok_dev, width = fwd_input.shape[1:]
    top_k = fwd_routes.shape[2]
    capacity = min(tok_dev, 2 * tok_dev * top_k // groups)
    slots = groups * capacity
    x_fwd, x_back, cot = fwd_input[0], back_input[0], cot_input[0]
    wg, wu, wd = w_gate[0, 0], w_up[0, 0], w_down[0, 0]
    head = verdict_head[None]

    def bind(kernel):
        def bound(*refs):
            kernel(groups, capacity, *refs)

        return bound

    def exchange(value):
        return lax.all_to_all(value, "expert", split_axis=0, concat_axis=0, tiled=True)

    def move(value, dz, dx):
        return lax.ppermute(
            value,
            "expert",
            [
                (source, ((source + 2 * dz) % groups) ^ dx)
                for source in range(groups)
            ],
        )

    half = tok_dev // 2

    def along_z(value):
        below, above = move(value, 1, 0), move(value, -1, 0)
        return below, above

    def far_along_z(below, above):
        return move(below[:half], 1, 0), move(above[half:], -1, 0)

    mine = lax.axis_index("expert")
    is_last = lax.axis_index("section") == sections - 1
    place = jnp.stack([is_last.astype(jnp.int32), mine])
    below_f, above_f = along_z(x_fwd)
    pair_cot = move(cot, 0, 1)
    below_f, above_f, pair_cot = lax.optimization_barrier((below_f, above_f, pair_cot))
    x_sel = jnp.where(is_last, x_fwd, x_back)
    fields = jnp.concatenate(
        [
            fwd_routes[0].T.astype(f32),
            jnp.where(is_last, fwd_routes[0], back_routes[0]).T.astype(f32),
            jnp.where(is_last, fwd_gates[0], back_gates[0]).T,
            jnp.zeros((2, tok_dev), f32),
        ],
        axis=0,
    )
    fields = exchange(jnp.broadcast_to(fields[None], (groups,) + fields.shape))
    order = jnp.stack(sources(mine))
    fields = jnp.take(fields, order[:5], axis=0).transpose(0, 2, 1)
    ids_f = fields[:4, :, 0:2].astype(jnp.int32)
    ids_b = fields[:4, :, 2:4].astype(jnp.int32)
    ids_d = fields[0::4, :, 2:4].astype(jnp.int32)
    gates_d = fields[0::4, :, 4:6]

    def picked(own, below, above, far, ids):
        return call(
            bind(pick_rows),
            "pick_rows",
            [((slots // 2, width), bf16)] * 2,
            (place, own, below, above, *far, norm_gain, ids),
            [smem] + [vmem] * 7,
        )

    far_f = far_along_z(below_f, above_f)
    below_f, above_f, x_ring = lax.optimization_barrier((below_f, above_f, x_sel))
    below_b, above_b = along_z(x_ring)
    near_f, other_f = picked(x_fwd, below_f, above_f, far_f, ids_f)
    other_f = move(other_f, 0, 1)
    send_d = call(
        bind(weigh_rows),
        "weigh_rows",
        [((2 * capacity, width), bf16)] * 4,
        (place, cot, pair_cot, head, ids_d, gates_d),
        [smem] + [vmem] * 5,
    )
    far_b = far_along_z(below_b, above_b)
    below_b, above_b, send_d = lax.optimization_barrier((below_b, above_b, send_d))
    got_d = [move(send_d[step % 4], step, 0) if step else send_d[0] for step in (0, 1, 3, 2)]
    near_b, other_b = picked(x_sel, below_b, above_b, far_b, ids_b)
    other_b = move(other_b, 0, 1)

    rows_f = jnp.concatenate([near_f, other_f], axis=0)
    gate_pre = jnp.dot(rows_f, wg, preferred_element_type=f32)
    up_pre = jnp.dot(rows_f, wu, preferred_element_type=f32)
    hidden_f = (jax.nn.silu(gate_pre) * up_pre).astype(bf16)
    out_f = jnp.dot(hidden_f, wd, preferred_element_type=f32).astype(bf16)
    ret_send, dots = call(
        bind(attach_dots),
        "attach_dots",
        [((groups, capacity, width + extra), bf16), ((groups, 1, capacity), f32)],
        (place, out_f, head),
        [smem, vmem, vmem],
    )
    dots = exchange(dots)
    last_block = pl.BlockSpec((slots, extra), lambda i: (0, width // extra))
    coef, ret_send = call(
        bind(find_coefs),
        "find_coefs",
        [((tok_dev, 1), f32), ((slots, width + extra), bf16)],
        (
            place,
            x_fwd,
            fwd_routes[0],
            fwd_gates[0],
            head,
            verdict_labels[:, None],
            dots,
            ret_send.reshape(slots, width + extra),
        ),
        [smem] + [vmem] * 6 + [last_block],
        out_specs=[vmem, last_block],
        aliases={7: 1},
    )
    got_d, other_b, ret_send = lax.optimization_barrier((got_d, other_b, ret_send))
    ret_f = exchange(ret_send.reshape(groups, capacity, width + extra))
    ret_f = ret_f.reshape(slots, width + extra)
    rows_b = jnp.concatenate([near_b, other_b], axis=0)
    rows_d = jnp.concatenate(
        [block[:capacity] for block in got_d] + [block[capacity:] for block in got_d], axis=0
    )

    gate_pre = jnp.dot(rows_b, wg, preferred_element_type=f32)
    up_pre = jnp.dot(rows_b, wu, preferred_element_type=f32)
    sig = jax.nn.sigmoid(gate_pre)
    silu = gate_pre * sig
    hidden_b = (silu * up_pre).astype(bf16)
    d_hidden = contract_cols(rows_d, wd)
    d_gate = (d_hidden * up_pre * sig * (1.0 + gate_pre * (1.0 - sig))).astype(bf16)
    d_up = (d_hidden * silu).astype(bf16)
    d_rows = (contract_cols(d_gate, wg) + contract_cols(d_up, wu)).astype(bf16)

    (d_rows,) = call(
        bind(split_rows),
        "split_rows",
        [((groups, capacity, width), bf16)],
        (place, d_rows),
        [smem, vmem],
    )
    ret_f, d_rows = lax.optimization_barrier((ret_f, d_rows))
    ret_d = exchange(d_rows).reshape(slots, width)
    (layer_out,) = call(
        bind(join_forward),
        "join_forward",
        [((tok_dev, width), bf16)],
        (ret_f, x_fwd, fwd_routes[0], fwd_gates[0]),
        [vmem] * 4,
    )
    next_input = passed_along(layer_out, "section", 1)
    coef_rows = jnp.sum(ret_f[:, width:].astype(f32), axis=1).reshape(groups, capacity)
    coef_rows = jnp.take(coef_rows, order, axis=0).reshape(slots, 1)

    def scaled(value):
        return (value.astype(f32) * coef_rows).astype(bf16)

    grad_d = contract_rows(scaled(hidden_b), rows_d).astype(bf16)
    grad_g = contract_rows(rows_b, scaled(d_gate)).astype(bf16)
    grad_u = contract_rows(rows_b, scaled(d_up)).astype(bf16)

    ret_d, grad_d, grad_g, grad_u = lax.optimization_barrier((ret_d, grad_d, grad_g, grad_u))
    d_input, gain_local = call(
        bind(join_backward),
        "join_backward",
        [((tok_dev, width), bf16), ((1, width), f32)],
        (place, ret_d, x_sel, cot, coef, norm_gain, head, fwd_routes[0], back_routes[0]),
        [smem] + [vmem] * 8,
        [pltpu.VMEM((tok_dev, width), f32)],
    )
    prev_grad = passed_along(d_input, "section", -1)
    (next_input,) = call(
        copy_rows, "copy_rows", [((tok_dev, width), bf16)], (next_input, gain_local), [vmem] * 2
    )
    shares = lax.all_to_all(
        jnp.broadcast_to(gain_local[None], (groups, 1, width)),
        "expert",
        split_axis=0,
        concat_axis=0,
        tiled=True,
    )
    gain_grad = jnp.sum(shares, axis=0)
    return (
        next_input[None],
        prev_grad[None],
        gain_grad,
        grad_g[None, None],
        grad_u[None, None],
        grad_d[None, None],
    )


def solution(mesh):
    return jax.shard_map(
        on_device,
        mesh=mesh,
        in_specs=(
            P("section", "expert", None),
            P("section", "expert", None),
            P("section", "expert", None),
            P("section", "expert", None),
            P("section", "expert", None),
            P("section", "expert", None),
            P("section", "expert", None),
            P("section", "expert", None, None),
            P("section", "expert", None, None),
            P("section", "expert", None, None),
            P("section", None),
            P(),
            P("expert"),
        ),
        out_specs=(
            P("section", "expert", None),
            P("section", "expert", None),
            P("section", None),
            P("section", "expert", None, None),
            P("section", "expert", None, None),
            P("section", "expert", None, None),
        ),
        check_vma=False,
    )
```

```python
import functools
import math

import jax
import jax.numpy as jnp
from jax import lax
from jax.experimental import pallas as pl
from jax.experimental.pallas import tpu as pltpu
from jax.sharding import PartitionSpec as P

loss_scale = 64.0
norm_eps = 1e-06
bf16 = jnp.bfloat16
f32 = jnp.float32
chunk = 512
extra = 128
steps = (0, -1, 1, 2)
vmem = pl.BlockSpec(memory_space=pltpu.VMEM)
smem = pl.BlockSpec(memory_space=pltpu.SMEM)
anywhere = pl.BlockSpec(memory_space=pl.ANY)


def passed_along(value, axis, steps):
    count = lax.axis_size(axis)
    initial, last = (max(0, -steps), min(count, count - steps))
    return lax.ppermute(value, axis, [(source, source + steps) for source in range(initial, last)])


def slot_keys(ids, groups, capacity):
    tokens = ids.shape[0]
    lanes = lax.broadcasted_iota(jnp.int32, (tokens, 128), 1)
    hit0 = ids[:, 0:1] == lanes
    hit1 = ids[:, 1:2] == lanes
    hits = (hit0 | hit1).astype(bf16)
    before = (
        lax.broadcasted_iota(jnp.int32, (tokens, tokens), 1)
        < lax.broadcasted_iota(jnp.int32, (tokens, tokens), 0)
    ).astype(bf16)
    ranks = jnp.dot(before, hits, preferred_element_type=f32)
    rank0 = jnp.sum(jnp.where(hit0, ranks, 0.0), axis=1, keepdims=True).astype(jnp.int32)
    rank1 = jnp.sum(jnp.where(hit1, ranks, 0.0), axis=1, keepdims=True).astype(jnp.int32)
    return ids[:, 0:1] * capacity + rank0, ids[:, 1:2] * capacity + rank1


def slot_hits(ids, groups, capacity):
    key0, key1 = slot_keys(ids, groups, capacity)
    slots = lax.broadcasted_iota(jnp.int32, (ids.shape[0], groups * capacity), 1)
    return key0 == slots, key1 == slots


def split_weights(hit0, hit1, gates):
    weights = jnp.where(hit0, gates[:, 0:1], 0.0) + jnp.where(hit1, gates[:, 1:2], 0.0)
    high = weights.astype(bf16)
    low = (weights - high.astype(f32)).astype(bf16)
    return high, low


def over_tokens(left, right):
    return lax.dot_general(left, right, (((0,), (0,)), ((), ())), preferred_element_type=f32)


def over_chunks(width, body, carry=None):
    for at in range(0, width, chunk):
        carry = body(slice(at, at + chunk), carry)
    return carry


def loop_chunks(width, body, carry):
    def step(at, carry):
        return body(pl.ds(pl.multiple_of(at * chunk, chunk), chunk), carry)

    return lax.fori_loop(0, width // chunk, step, carry)


def columns(table):
    return table.T


def as_ids(pair):
    return pair.astype(jnp.int32)


def ranked(hit):
    tokens = hit.shape[0]
    before = (
        lax.broadcasted_iota(jnp.int32, (tokens, tokens), 1)
        < lax.broadcasted_iota(jnp.int32, (tokens, tokens), 0)
    ).astype(bf16)
    return jnp.dot(before, hit.astype(bf16), preferred_element_type=f32).astype(jnp.int32)


def pick_rows(
    field,
    groups,
    capacity,
    place_ref,
    table_ref,
    own_ref,
    below_ref,
    above_ref,
    far_low_ref,
    far_high_ref,
    gain_ref,
    near_ref,
    other_ref,
):
    mine = place_ref[1]
    tokens, width = own_ref.shape
    lanes = lax.broadcasted_iota(jnp.int32, (tokens, 2 * capacity), 1)
    wanted = jnp.where(lanes < capacity, mine, mine ^ 1)

    def far(cols):
        return jnp.concatenate([far_low_ref[:, cols], far_high_ref[:, cols]], axis=0)

    readers = (
        lambda cols: own_ref[:, cols],
        lambda cols: below_ref[:, cols],
        lambda cols: above_ref[:, cols],
        far,
    )
    picks = []
    for source in sources(mine)[:4]:
        ids = as_ids(columns(table_ref[source])[:, field : field + 2])
        hit = (ids[:, 0:1] == wanted) | (ids[:, 1:2] == wanted)
        picks.append((hit & (ranked(hit) == (lanes & (capacity - 1)))).astype(bf16))

    def square(cols, totals):
        rows = [read(cols).astype(f32) for read in readers]
        return tuple(
            total + jnp.sum(x * x, axis=1, keepdims=True) for total, x in zip(totals, rows)
        )

    totals = loop_chunks(width, square, (jnp.zeros((tokens, 1), f32),) * 4)
    invs = [lax.rsqrt(total / width + norm_eps) for total in totals]

    def fill(cols, carry):
        for at, read in enumerate(readers):
            normed = (read(cols).astype(f32) * invs[at] * gain_ref[:, cols]).astype(bf16)
            got = over_tokens(picks[at], normed).astype(bf16)
            place = slice(at * capacity, (at + 1) * capacity)
            near_ref[place, cols] = got[:capacity]
            other_ref[place, cols] = got[capacity:]
        return carry

    loop_chunks(width, fill, 0)


def weigh_rows(groups, capacity, place_ref, table_ref, own_ref, pair_ref, head_ref, *out_refs):
    is_last = place_ref[0] == 1
    mine = place_ref[1]
    tokens, width = own_ref.shape
    lanes = lax.broadcasted_iota(jnp.int32, (tokens, len(out_refs) * capacity), 1)
    wanted = (mine + 2 * lax.div(lanes, capacity)) & (groups - 1)
    weights = []
    for side in range(2):
        fields = columns(table_ref[mine ^ side])
        ids = as_ids(fields[:, 2:4])
        hit0, hit1 = ids[:, 0:1] == wanted, ids[:, 1:2] == wanted
        inside = ranked(hit0 | hit1) == (lanes & (capacity - 1))
        weights.append(split_weights(hit0 & inside, hit1 & inside, fields[:, 4:6]))

    def fill(cols, carry):
        for side, cot_ref in enumerate((own_ref, pair_ref)):
            high, low = weights[side]
            cot = cot_ref[:, cols]
            head = jnp.broadcast_to(head_ref[:, cols], cot.shape)
            head_high = head.astype(bf16)
            head_low = (head - head_high.astype(f32)).astype(bf16)
            cot_high = jnp.where(is_last, head_high.astype(f32), cot.astype(f32)).astype(bf16)
            cot_low = jnp.where(is_last, head_low.astype(f32), 0.0).astype(bf16)
            dout = (
                over_tokens(high, cot_high) + over_tokens(low, cot_high) + over_tokens(high, cot_low)
            ).astype(bf16)
            for at, ref in enumerate(out_refs):
                ref[side * capacity : (side + 1) * capacity, cols] = dout[
                    at * capacity : (at + 1) * capacity
                ]
        return carry

    loop_chunks(width, fill, 0)


def in_parts(column):
    lanes = lax.broadcasted_iota(jnp.int32, (column.shape[0], extra), 1)
    out = jnp.zeros((column.shape[0], extra), f32)
    rest = column
    for lane in range(3):
        part = rest.astype(bf16).astype(f32)
        out = jnp.where(lanes == lane, part, out)
        rest = rest - part
    return out.astype(bf16)


def sources(mine):
    return [((mine + 2 * (step + 4)) & 7) ^ side for side in (0, 1) for step in steps]


def attach_dots(groups, capacity, place_ref, out_ref, head_ref, ret_ref, dots_ref):
    width = out_ref.shape[1]
    rows = lax.broadcasted_iota(jnp.int32, (8, width), 0)
    parts = jnp.zeros((8, width), f32)
    rest = head_ref[...]
    for row in range(3):
        part = rest.astype(bf16).astype(f32)
        parts = jnp.where(rows == row, part, parts)
        rest = rest - part
    parts = parts.astype(bf16)
    for at, source in enumerate(sources(place_ref[1])):
        out = out_ref[at * capacity : (at + 1) * capacity, :]
        ret_ref[source, :, :width] = out
        ret_ref[source, :, width:] = jnp.zeros((capacity, extra), bf16)
        dots = lax.dot_general(parts, out, (((1,), (1,)), ((), ())), preferred_element_type=f32)
        dots_ref[source] = jnp.sum(dots, axis=0, keepdims=True)


def split_rows(groups, capacity, place_ref, in_ref, out_ref):
    for at, source in enumerate(sources(place_ref[1])):
        out_ref[source] = in_ref[at * capacity : (at + 1) * capacity, :]


def find_coefs(
    groups,
    capacity,
    place_ref,
    table_ref,
    x_ref,
    head_ref,
    labels_ref,
    dots_ref,
    unused_ref,
    coef_ref,
    block_ref,
):
    is_last = place_ref[0] == 1
    fields = columns(table_ref[...])
    hit0, hit1 = slot_hits(as_ids(fields[:, 0:2]), groups, capacity)
    pick = (hit0 | hit1).astype(bf16)
    weights = jnp.where(hit0, fields[:, 6:7], 0.0) + jnp.where(hit1, fields[:, 7:8], 0.0)

    def add(cols, logits):
        return logits + jnp.sum(
            x_ref[:, cols].astype(f32) * head_ref[:, cols], axis=1, keepdims=True
        )

    logits = over_chunks(x_ref.shape[1], add, jnp.zeros((x_ref.shape[0], 1), f32))
    for at in range(groups):
        block = weights[:, at * capacity : (at + 1) * capacity]
        logits += jnp.sum(block * dots_ref[at], axis=1, keepdims=True)
    coef = loss_scale * (jax.nn.sigmoid(logits) - labels_ref[...].astype(f32))
    coef = jnp.where(is_last, coef, 1.0)
    coef_ref[...] = coef
    picked = over_tokens(pick, in_parts(coef))
    ones = (lax.broadcasted_iota(jnp.int32, picked.shape, 1) == 0).astype(f32)
    block_ref[...] = jnp.where(is_last, picked, ones).astype(bf16)


def join_forward(groups, capacity, table_ref, ret_ref, x_ref, out_ref):
    fields = columns(table_ref[...])
    hit0, hit1 = slot_hits(as_ids(fields[:, 0:2]), groups, capacity)
    high, low = split_weights(hit0, hit1, fields[:, 6:8])

    def fill(cols, carry):
        ret = ret_ref[:, cols]
        mixed = jnp.dot(high, ret, preferred_element_type=f32) + jnp.dot(
            low, ret, preferred_element_type=f32
        )
        out_ref[:, cols] = (x_ref[:, cols].astype(f32) + mixed).astype(bf16)
        return carry

    loop_chunks(x_ref.shape[1], fill, 0)


def copy_rows(in_ref, unused_ref, out_ref):
    out_ref[...] = in_ref[...]


def assemble(pieces, *refs):
    sources_refs, out_ref, sems = refs[:-2], refs[-2], refs[-1]
    copies = []
    for at, (which, start, rows, to) in enumerate(pieces):
        copy = pltpu.make_async_copy(
            sources_refs[which].at[pl.ds(start, rows)], out_ref.at[pl.ds(to, rows)], sems.at[at]
        )
        copy.start()
        copies.append(copy)
    for copy in copies:
        copy.wait()


def join_backward(
    groups,
    capacity,
    place_ref,
    table_ref,
    ret_ref,
    x_ref,
    cot_ref,
    coef_ref,
    gain_ref,
    head_ref,
    out_ref,
    grad_ref,
    normed_ref,
):
    is_last = place_ref[0] == 1
    fields = columns(table_ref[...])
    hit0, hit1 = slot_hits(as_ids(fields[:, 2:4]), groups, capacity)
    pick = (hit0 | hit1).astype(bf16)
    coef = coef_ref[...]
    tokens, width = x_ref.shape
    zero = jnp.zeros((tokens, 1), f32)

    def square(cols, total):
        x = x_ref[:, cols].astype(f32)
        return total + jnp.sum(x * x, axis=1, keepdims=True)

    inv = lax.rsqrt(over_chunks(width, square, zero) / width + norm_eps)

    def first(cols, dots):
        d_normed = coef * jnp.dot(pick, ret_ref[:, cols], preferred_element_type=f32)
        normed_ref[:, cols] = d_normed
        product = d_normed * x_ref[:, cols].astype(f32)
        grad_ref[:, cols] = jnp.sum(product * inv, axis=0, keepdims=True)
        return dots + jnp.sum(product * gain_ref[:, cols], axis=1, keepdims=True)

    scale = inv * inv * inv * (over_chunks(width, first, zero) / width)

    def second(cols, carry):
        cot = jnp.where(is_last, coef * head_ref[:, cols], cot_ref[:, cols].astype(f32))
        out_ref[:, cols] = (
            cot
            + inv * (gain_ref[:, cols] * normed_ref[:, cols])
            - x_ref[:, cols].astype(f32) * scale
        ).astype(bf16)
        return carry

    over_chunks(width, second, 0)


def call(kernel, name, outs, args, specs, scratch=(), out_specs=None, aliases=None, flops=0):
    moved = sum(value.size * value.dtype.itemsize for value in args)
    moved += sum(math.prod(shape) * jnp.dtype(dtype).itemsize for shape, dtype in outs)
    return pl.pallas_call(
        kernel,
        cost_estimate=pl.CostEstimate(flops=flops, transcendentals=0, bytes_accessed=moved),
        out_shape=[jax.ShapeDtypeStruct(shape, dtype) for shape, dtype in outs],
        grid=(1,),
        in_specs=specs,
        out_specs=out_specs or [vmem] * len(outs),
        scratch_shapes=list(scratch),
        input_output_aliases=aliases or {},
        compiler_params=pltpu.CompilerParams(vmem_limit_bytes=48 << 20),
        name=name,
    )(*args)


def contract_rows(left_op, right_op):
    return lax.dot_general(
        left_op, right_op, (((0,), (0,)), ((), ())), preferred_element_type=f32
    )


def contract_cols(left_op, right_op):
    return lax.dot_general(
        left_op, right_op, (((1,), (1,)), ((), ())), preferred_element_type=f32
    )


def on_device(
    fwd_input,
    back_input,
    cot_input,
    fwd_routes,
    back_routes,
    fwd_gates,
    back_gates,
    w_gate,
    w_up,
    w_down,
    norm_gain,
    verdict_head,
    verdict_labels,
):
    sections = lax.axis_size("section")
    groups = lax.axis_size("expert")
    tok_dev, width = fwd_input.shape[1:]
    top_k = fwd_routes.shape[2]
    capacity = min(tok_dev, 2 * tok_dev * top_k // groups)
    slots = groups * capacity
    x_fwd, x_back, cot = fwd_input[0], back_input[0], cot_input[0]
    wg, wu, wd = w_gate[0, 0], w_up[0, 0], w_down[0, 0]
    head = verdict_head[None]

    def bind(kernel):
        def bound(*refs):
            kernel(groups, capacity, *refs)

        return bound

    def exchange(value):
        return lax.all_to_all(value, "expert", split_axis=0, concat_axis=0, tiled=True)

    def move(value, dz, dx):
        return lax.ppermute(
            value,
            "expert",
            [
                (source, ((source + 2 * dz) % groups) ^ dx)
                for source in range(groups)
            ],
        )

    half = tok_dev // 2

    def along_z(value):
        below, above = move(value, 1, 0), move(value, -1, 0)
        return below, above

    def far_along_z(below, above):
        return move(below[:half], 1, 0), move(above[half:], -1, 0)

    mine = lax.axis_index("expert")
    is_last = lax.axis_index("section") == sections - 1
    place = jnp.stack([is_last.astype(jnp.int32), mine])
    below_f, above_f = along_z(x_fwd)
    pair_cot = move(cot, 0, 1)
    below_f, above_f, pair_cot = lax.optimization_barrier((below_f, above_f, pair_cot))
    x_sel = jnp.where(is_last, x_fwd, x_back)
    table = jnp.concatenate(
        [
            fwd_routes[0].T.astype(f32),
            jnp.where(is_last, fwd_routes[0], back_routes[0]).T.astype(f32),
            jnp.where(is_last, fwd_gates[0], back_gates[0]).T,
            fwd_gates[0].T,
        ],
        axis=0,
    )
    tables = exchange(jnp.broadcast_to(table[None], (groups,) + table.shape))
    order = jnp.stack(sources(mine))

    def picked(field, own, below, above, far):
        return call(
            functools.partial(pick_rows, field, groups, capacity),
            "pick_rows",
            [((slots // 2, width), bf16)] * 2,
            (place, tables, own, below, above, *far, norm_gain),
            [smem] + [vmem] * 7,
            flops=4 * slots * tok_dev * width,
        )

    def assembled(blocks, pieces):
        return call(
            functools.partial(assemble, pieces),
            "assemble",
            [((slots, width), bf16)],
            blocks,
            [anywhere] * len(blocks),
            [pltpu.SemaphoreType.DMA((len(pieces),))],
            out_specs=[anywhere],
        )[0]

    far_f = far_along_z(below_f, above_f)
    tables, far_f = lax.optimization_barrier((tables, far_f))
    below_f, above_f, x_ring = lax.optimization_barrier((below_f, above_f, x_sel))
    below_b, above_b = along_z(x_ring)
    near_f, other_f = picked(0, x_fwd, below_f, above_f, far_f)
    other_f = move(other_f, 0, 1)
    send_d = call(
        bind(weigh_rows),
        "weigh_rows",
        [((2 * capacity, width), bf16)] * 4,
        (place, tables, cot, pair_cot, head),
        [smem] + [vmem] * 4,
        flops=8 * slots * tok_dev * width,
    )
    below_b, above_b, send_d = lax.optimization_barrier((below_b, above_b, send_d))
    far_b = far_along_z(below_b, above_b)
    near_b, other_b = picked(2, x_sel, below_b, above_b, far_b)
    other_b, send_d = lax.optimization_barrier((other_b, send_d))
    other_b = move(other_b, 0, 1)
    got_d = [move(send_d[step % 4], step, 0) if step else send_d[0] for step in (0, 1, 3, 2)]

    halves = [(0, 0, slots // 2, 0), (1, 0, slots // 2, slots // 2)]
    quarters = [
        (at, side * capacity, capacity, (side * 4 + at) * capacity)
        for side in range(2)
        for at in range(4)
    ]
    rows_f = assembled((near_f, other_f), halves)
    gate_pre = jnp.dot(rows_f, wg, preferred_element_type=f32)
    up_pre = jnp.dot(rows_f, wu, preferred_element_type=f32)
    hidden_f = lax.optimization_barrier((jax.nn.silu(gate_pre) * up_pre).astype(bf16))
    out_f = jnp.dot(hidden_f, wd, preferred_element_type=f32).astype(bf16)
    ret_send, dots = call(
        bind(attach_dots),
        "attach_dots",
        [((groups, capacity, width + extra), bf16), ((groups, 1, capacity), f32)],
        (place, out_f, head),
        [smem, vmem, vmem],
    )
    dots = exchange(dots)
    last_block = pl.BlockSpec((slots, extra), lambda i: (0, width // extra))
    coef, ret_send = call(
        bind(find_coefs),
        "find_coefs",
        [((tok_dev, 1), f32), ((slots, width + extra), bf16)],
        (
            place,
            table,
            x_fwd,
            head,
            verdict_labels[:, None],
            dots,
            ret_send.reshape(slots, width + extra),
        ),
        [smem] + [vmem] * 5 + [last_block],
        out_specs=[vmem, last_block],
        aliases={6: 1},
    )
    got_d, other_b, ret_send = lax.optimization_barrier((got_d, other_b, ret_send))
    ret_f = exchange(ret_send.reshape(groups, capacity, width + extra))
    ret_f = ret_f.reshape(slots, width + extra)
    rows_b = assembled((near_b, other_b), halves)
    rows_d = assembled(tuple(got_d), quarters)

    gate_pre = jnp.dot(rows_b, wg, preferred_element_type=f32)
    up_pre = jnp.dot(rows_b, wu, preferred_element_type=f32)
    sig = jax.nn.sigmoid(gate_pre)
    silu = gate_pre * sig
    hidden_b = (silu * up_pre).astype(bf16)
    d_hidden = contract_cols(rows_d, wd)
    d_gate = (d_hidden * up_pre * sig * (1.0 + gate_pre * (1.0 - sig))).astype(bf16)
    d_up = (d_hidden * silu).astype(bf16)
    d_rows = (contract_cols(d_gate, wg) + contract_cols(d_up, wu)).astype(bf16)

    (d_rows,) = call(
        bind(split_rows),
        "split_rows",
        [((groups, capacity, width), bf16)],
        (place, d_rows),
        [smem, vmem],
    )
    ret_f, d_rows = lax.optimization_barrier((ret_f, d_rows))
    ret_d = exchange(d_rows).reshape(slots, width)
    (layer_out,) = call(
        bind(join_forward),
        "join_forward",
        [((tok_dev, width), bf16)],
        (table, ret_f, x_fwd),
        [vmem] * 3,
    )
    next_input = passed_along(layer_out, "section", 1)
    coef_rows = jnp.sum(ret_f[:, width:].astype(f32), axis=1).reshape(groups, capacity)
    coef_rows = jnp.take(coef_rows, order, axis=0).reshape(slots, 1)

    def scaled(value):
        return (value.astype(f32) * coef_rows).astype(bf16)

    grad_d = contract_rows(scaled(hidden_b), rows_d).astype(bf16)
    grad_g = contract_rows(rows_b, scaled(d_gate)).astype(bf16)
    grad_u = contract_rows(rows_b, scaled(d_up)).astype(bf16)

    ret_d, grad_d, grad_g, grad_u = lax.optimization_barrier((ret_d, grad_d, grad_g, grad_u))
    d_input, gain_local = call(
        bind(join_backward),
        "join_backward",
        [((tok_dev, width), bf16), ((1, width), f32)],
        (place, table, ret_d, x_sel, cot, coef, norm_gain, head),
        [smem] + [vmem] * 7,
        [pltpu.VMEM((tok_dev, width), f32)],
    )
    prev_grad = passed_along(d_input, "section", -1)
    (next_input,) = call(
        copy_rows, "copy_rows", [((tok_dev, width), bf16)], (next_input, gain_local), [vmem] * 2
    )
    gain_grad = gain_local
    step = 1
    while step < groups:
        gain_grad = gain_grad + lax.ppermute(
            gain_grad, "expert", [(source, source ^ step) for source in range(groups)]
        )
        step *= 2
    return (
        next_input[None],
        prev_grad[None],
        gain_grad,
        grad_g[None, None],
        grad_u[None, None],
        grad_d[None, None],
    )


def solution(mesh):
    return jax.shard_map(
        on_device,
        mesh=mesh,
        in_specs=(
            P("section", "expert", None),
            P("section", "expert", None),
            P("section", "expert", None),
            P("section", "expert", None),
            P("section", "expert", None),
            P("section", "expert", None),
            P("section", "expert", None),
            P("section", "expert", None, None),
            P("section", "expert", None, None),
            P("section", "expert", None, None),
            P("section", None),
            P(),
            P("expert"),
        ),
        out_specs=(
            P("section", "expert", None),
            P("section", "expert", None),
            P("section", None),
            P("section", "expert", None, None),
            P("section", "expert", None, None),
            P("section", "expert", None, None),
        ),
        check_vma=False,
    )
```

```python
import functools
import math

import jax
import jax.numpy as jnp
from jax import lax
from jax.experimental import pallas as pl
from jax.experimental.pallas import tpu as pltpu
from jax.sharding import PartitionSpec as P

loss_scale = 64.0
norm_eps = 1e-06
bf16 = jnp.bfloat16
f32 = jnp.float32
chunk = 512
extra = 128
steps = (0, -1, 1, 2)
vmem = pl.BlockSpec(memory_space=pltpu.VMEM)
smem = pl.BlockSpec(memory_space=pltpu.SMEM)
anywhere = pl.BlockSpec(memory_space=pl.ANY)


def passed_along(value, axis, steps):
    count = lax.axis_size(axis)
    initial, last = (max(0, -steps), min(count, count - steps))
    return lax.ppermute(value, axis, [(source, source + steps) for source in range(initial, last)])


def slot_keys(ids, groups, capacity):
    tokens = ids.shape[0]
    lanes = lax.broadcasted_iota(jnp.int32, (tokens, 128), 1)
    hit0 = ids[:, 0:1] == lanes
    hit1 = ids[:, 1:2] == lanes
    hits = (hit0 | hit1).astype(bf16)
    before = (
        lax.broadcasted_iota(jnp.int32, (tokens, tokens), 1)
        < lax.broadcasted_iota(jnp.int32, (tokens, tokens), 0)
    ).astype(bf16)
    ranks = jnp.dot(before, hits, preferred_element_type=f32)
    rank0 = jnp.sum(jnp.where(hit0, ranks, 0.0), axis=1, keepdims=True).astype(jnp.int32)
    rank1 = jnp.sum(jnp.where(hit1, ranks, 0.0), axis=1, keepdims=True).astype(jnp.int32)
    return ids[:, 0:1] * capacity + rank0, ids[:, 1:2] * capacity + rank1


def slot_hits(ids, groups, capacity):
    key0, key1 = slot_keys(ids, groups, capacity)
    slots = lax.broadcasted_iota(jnp.int32, (ids.shape[0], groups * capacity), 1)
    return key0 == slots, key1 == slots


def split_weights(hit0, hit1, gates):
    weights = jnp.where(hit0, gates[:, 0:1], 0.0) + jnp.where(hit1, gates[:, 1:2], 0.0)
    high = weights.astype(bf16)
    low = (weights - high.astype(f32)).astype(bf16)
    return high, low


def over_tokens(left, right):
    return lax.dot_general(left, right, (((0,), (0,)), ((), ())), preferred_element_type=f32)


def over_chunks(width, body, carry=None):
    for at in range(0, width, chunk):
        carry = body(slice(at, at + chunk), carry)
    return carry


def loop_chunks(width, body, carry):
    def step(at, carry):
        return body(pl.ds(pl.multiple_of(at * chunk, chunk), chunk), carry)

    return lax.fori_loop(0, width // chunk, step, carry)


def columns(table):
    return table.T


def as_ids(pair):
    return pair.astype(jnp.int32)


def ranked(hit):
    tokens = hit.shape[0]
    before = (
        lax.broadcasted_iota(jnp.int32, (tokens, tokens), 1)
        < lax.broadcasted_iota(jnp.int32, (tokens, tokens), 0)
    ).astype(bf16)
    return jnp.dot(before, hit.astype(bf16), preferred_element_type=f32).astype(jnp.int32)


def pick_rows(
    field,
    groups,
    capacity,
    place_ref,
    table_ref,
    own_ref,
    below_ref,
    above_ref,
    far_low_ref,
    far_high_ref,
    gain_ref,
    near_ref,
    other_ref,
):
    mine = place_ref[1]
    tokens, width = own_ref.shape
    lanes = lax.broadcasted_iota(jnp.int32, (tokens, 2 * capacity), 1)
    wanted = jnp.where(lanes < capacity, mine, mine ^ 1)

    def far(cols):
        return jnp.concatenate([far_low_ref[:, cols], far_high_ref[:, cols]], axis=0)

    readers = (
        lambda cols: own_ref[:, cols],
        lambda cols: below_ref[:, cols],
        lambda cols: above_ref[:, cols],
        far,
    )
    picks = []
    for source in sources(mine)[:4]:
        ids = as_ids(columns(table_ref[source])[:, field : field + 2])
        hit = (ids[:, 0:1] == wanted) | (ids[:, 1:2] == wanted)
        picks.append((hit & (ranked(hit) == (lanes & (capacity - 1)))).astype(bf16))

    def square(cols, totals):
        rows = [read(cols).astype(f32) for read in readers]
        return tuple(
            total + jnp.sum(x * x, axis=1, keepdims=True) for total, x in zip(totals, rows)
        )

    totals = loop_chunks(width, square, (jnp.zeros((tokens, 1), f32),) * 4)
    invs = [lax.rsqrt(total / width + norm_eps) for total in totals]

    def fill(cols, carry):
        for at, read in enumerate(readers):
            normed = (read(cols).astype(f32) * invs[at] * gain_ref[:, cols]).astype(bf16)
            got = over_tokens(picks[at], normed).astype(bf16)
            place = slice(at * capacity, (at + 1) * capacity)
            near_ref[place, cols] = got[:capacity]
            other_ref[place, cols] = got[capacity:]
        return carry

    loop_chunks(width, fill, 0)


def weigh_rows(groups, capacity, place_ref, table_ref, own_ref, pair_ref, head_ref, *out_refs):
    is_last = place_ref[0] == 1
    mine = place_ref[1]
    tokens, width = own_ref.shape
    lanes = lax.broadcasted_iota(jnp.int32, (tokens, len(out_refs) * capacity), 1)
    wanted = (mine + 2 * lax.div(lanes, capacity)) & (groups - 1)
    weights = []
    for side in range(2):
        fields = columns(table_ref[mine ^ side])
        ids = as_ids(fields[:, 2:4])
        hit0, hit1 = ids[:, 0:1] == wanted, ids[:, 1:2] == wanted
        inside = ranked(hit0 | hit1) == (lanes & (capacity - 1))
        weights.append(split_weights(hit0 & inside, hit1 & inside, fields[:, 4:6]))

    def fill(cols, carry):
        for side, cot_ref in enumerate((own_ref, pair_ref)):
            high, low = weights[side]
            cot = cot_ref[:, cols]
            head = jnp.broadcast_to(head_ref[:, cols], cot.shape)
            head_high = head.astype(bf16)
            head_low = (head - head_high.astype(f32)).astype(bf16)
            cot_high = jnp.where(is_last, head_high.astype(f32), cot.astype(f32)).astype(bf16)
            cot_low = jnp.where(is_last, head_low.astype(f32), 0.0).astype(bf16)
            dout = (
                over_tokens(high, cot_high) + over_tokens(low, cot_high) + over_tokens(high, cot_low)
            ).astype(bf16)
            for at, ref in enumerate(out_refs):
                ref[side * capacity : (side + 1) * capacity, cols] = dout[
                    at * capacity : (at + 1) * capacity
                ]
        return carry

    loop_chunks(width, fill, 0)


def in_parts(column):
    lanes = lax.broadcasted_iota(jnp.int32, (column.shape[0], extra), 1)
    out = jnp.zeros((column.shape[0], extra), f32)
    rest = column
    for lane in range(3):
        part = rest.astype(bf16).astype(f32)
        out = jnp.where(lanes == lane, part, out)
        rest = rest - part
    return out.astype(bf16)


def sources(mine):
    return [((mine + 2 * (step + 4)) & 7) ^ side for side in (0, 1) for step in steps]


def attach_dots(groups, capacity, place_ref, out_ref, head_ref, ret_ref, dots_ref):
    width = out_ref.shape[1]
    rows = lax.broadcasted_iota(jnp.int32, (8, width), 0)
    parts = jnp.zeros((8, width), f32)
    rest = head_ref[...]
    for row in range(3):
        part = rest.astype(bf16).astype(f32)
        parts = jnp.where(rows == row, part, parts)
        rest = rest - part
    parts = parts.astype(bf16)
    for at, source in enumerate(sources(place_ref[1])):
        out = out_ref[at * capacity : (at + 1) * capacity, :]
        ret_ref[source, :, :width] = out
        ret_ref[source, :, width:] = jnp.zeros((capacity, extra), bf16)
        dots = lax.dot_general(parts, out, (((1,), (1,)), ((), ())), preferred_element_type=f32)
        dots_ref[source] = jnp.sum(dots, axis=0, keepdims=True)


def split_rows(groups, capacity, place_ref, in_ref, out_ref):
    for at, source in enumerate(sources(place_ref[1])):
        out_ref[source] = in_ref[at * capacity : (at + 1) * capacity, :]


def find_coefs(
    groups,
    capacity,
    place_ref,
    table_ref,
    x_ref,
    head_ref,
    labels_ref,
    dots_ref,
    unused_ref,
    coef_ref,
    block_ref,
):
    is_last = place_ref[0] == 1
    fields = columns(table_ref[...])
    hit0, hit1 = slot_hits(as_ids(fields[:, 0:2]), groups, capacity)
    pick = (hit0 | hit1).astype(bf16)
    weights = jnp.where(hit0, fields[:, 6:7], 0.0) + jnp.where(hit1, fields[:, 7:8], 0.0)

    def add(cols, logits):
        return logits + jnp.sum(
            x_ref[:, cols].astype(f32) * head_ref[:, cols], axis=1, keepdims=True
        )

    logits = over_chunks(x_ref.shape[1], add, jnp.zeros((x_ref.shape[0], 1), f32))
    for at in range(groups):
        block = weights[:, at * capacity : (at + 1) * capacity]
        logits += jnp.sum(block * dots_ref[at], axis=1, keepdims=True)
    coef = loss_scale * (jax.nn.sigmoid(logits) - labels_ref[...].astype(f32))
    coef = jnp.where(is_last, coef, 1.0)
    coef_ref[...] = coef
    picked = over_tokens(pick, in_parts(coef))
    ones = (lax.broadcasted_iota(jnp.int32, picked.shape, 1) == 0).astype(f32)
    block_ref[...] = jnp.where(is_last, picked, ones).astype(bf16)


def join_forward(groups, capacity, table_ref, ret_ref, x_ref, out_ref):
    fields = columns(table_ref[...])
    hit0, hit1 = slot_hits(as_ids(fields[:, 0:2]), groups, capacity)
    high, low = split_weights(hit0, hit1, fields[:, 6:8])

    def fill(cols, carry):
        ret = ret_ref[:, cols]
        mixed = jnp.dot(high, ret, preferred_element_type=f32) + jnp.dot(
            low, ret, preferred_element_type=f32
        )
        out_ref[:, cols] = (x_ref[:, cols].astype(f32) + mixed).astype(bf16)
        return carry

    loop_chunks(x_ref.shape[1], fill, 0)


def copy_rows(in_ref, unused_ref, out_ref):
    out_ref[...] = in_ref[...]


def assemble(pieces, *refs):
    sources_refs, out_ref, sems = refs[:-2], refs[-2], refs[-1]
    copies = []
    for at, (which, start, rows, to) in enumerate(pieces):
        copy = pltpu.make_async_copy(
            sources_refs[which].at[pl.ds(start, rows)], out_ref.at[pl.ds(to, rows)], sems.at[at]
        )
        copy.start()
        copies.append(copy)
    for copy in copies:
        copy.wait()


def join_backward(
    groups,
    capacity,
    place_ref,
    table_ref,
    ret_ref,
    x_ref,
    cot_ref,
    coef_ref,
    gain_ref,
    head_ref,
    out_ref,
    grad_ref,
    normed_ref,
):
    is_last = place_ref[0] == 1
    fields = columns(table_ref[...])
    hit0, hit1 = slot_hits(as_ids(fields[:, 2:4]), groups, capacity)
    pick = (hit0 | hit1).astype(bf16)
    coef = coef_ref[...]
    tokens, width = x_ref.shape
    zero = jnp.zeros((tokens, 1), f32)

    def square(cols, total):
        x = x_ref[:, cols].astype(f32)
        return total + jnp.sum(x * x, axis=1, keepdims=True)

    inv = lax.rsqrt(over_chunks(width, square, zero) / width + norm_eps)

    def first(cols, dots):
        d_normed = coef * jnp.dot(pick, ret_ref[:, cols], preferred_element_type=f32)
        normed_ref[:, cols] = d_normed
        product = d_normed * x_ref[:, cols].astype(f32)
        grad_ref[:, cols] = jnp.sum(product * inv, axis=0, keepdims=True)
        return dots + jnp.sum(product * gain_ref[:, cols], axis=1, keepdims=True)

    scale = inv * inv * inv * (over_chunks(width, first, zero) / width)

    def second(cols, carry):
        cot = jnp.where(is_last, coef * head_ref[:, cols], cot_ref[:, cols].astype(f32))
        out_ref[:, cols] = (
            cot
            + inv * (gain_ref[:, cols] * normed_ref[:, cols])
            - x_ref[:, cols].astype(f32) * scale
        ).astype(bf16)
        return carry

    over_chunks(width, second, 0)


def call(kernel, name, outs, args, specs, scratch=(), out_specs=None, aliases=None, flops=0):
    moved = sum(value.size * value.dtype.itemsize for value in args)
    moved += sum(math.prod(shape) * jnp.dtype(dtype).itemsize for shape, dtype in outs)
    return pl.pallas_call(
        kernel,
        cost_estimate=pl.CostEstimate(flops=flops, transcendentals=0, bytes_accessed=moved),
        out_shape=[jax.ShapeDtypeStruct(shape, dtype) for shape, dtype in outs],
        grid=(1,),
        in_specs=specs,
        out_specs=out_specs or [vmem] * len(outs),
        scratch_shapes=list(scratch),
        input_output_aliases=aliases or {},
        compiler_params=pltpu.CompilerParams(vmem_limit_bytes=48 << 20),
        name=name,
    )(*args)


def contract_rows(left_op, right_op):
    return lax.dot_general(
        left_op, right_op, (((0,), (0,)), ((), ())), preferred_element_type=f32
    )


def contract_cols(left_op, right_op):
    return lax.dot_general(
        left_op, right_op, (((1,), (1,)), ((), ())), preferred_element_type=f32
    )


def on_device(
    fwd_input,
    back_input,
    cot_input,
    fwd_routes,
    back_routes,
    fwd_gates,
    back_gates,
    w_gate,
    w_up,
    w_down,
    norm_gain,
    verdict_head,
    verdict_labels,
):
    sections = lax.axis_size("section")
    groups = lax.axis_size("expert")
    tok_dev, width = fwd_input.shape[1:]
    top_k = fwd_routes.shape[2]
    capacity = min(tok_dev, 2 * tok_dev * top_k // groups)
    slots = groups * capacity
    x_fwd, x_back, cot = fwd_input[0], back_input[0], cot_input[0]
    wg, wu, wd = w_gate[0, 0], w_up[0, 0], w_down[0, 0]
    head = verdict_head[None]

    def bind(kernel):
        def bound(*refs):
            kernel(groups, capacity, *refs)

        return bound

    def exchange(value):
        return lax.all_to_all(value, "expert", split_axis=0, concat_axis=0, tiled=True)

    def move(value, dz, dx):
        return lax.ppermute(
            value,
            "expert",
            [
                (source, ((source + 2 * dz) % groups) ^ dx)
                for source in range(groups)
            ],
        )

    half = tok_dev // 2

    def along_z(value):
        below, above = move(value, 1, 0), move(value, -1, 0)
        return below, above

    def far_along_z(below, above):
        return move(below[:half], 1, 0), move(above[half:], -1, 0)

    mine = lax.axis_index("expert")
    is_last = lax.axis_index("section") == sections - 1
    place = jnp.stack([is_last.astype(jnp.int32), mine])
    below_f, above_f = along_z(x_fwd)
    pair_cot = move(cot, 0, 1)
    below_f, above_f, pair_cot = lax.optimization_barrier((below_f, above_f, pair_cot))
    x_sel = jnp.where(is_last, x_fwd, x_back)
    table = jnp.concatenate(
        [
            fwd_routes[0].T.astype(f32),
            jnp.where(is_last, fwd_routes[0], back_routes[0]).T.astype(f32),
            jnp.where(is_last, fwd_gates[0], back_gates[0]).T,
            fwd_gates[0].T,
        ],
        axis=0,
    )
    tables = exchange(jnp.broadcast_to(table[None], (groups,) + table.shape))
    order = jnp.stack(sources(mine))

    def picked(field, own, below, above, far):
        return call(
            functools.partial(pick_rows, field, groups, capacity),
            "pick_rows",
            [((slots // 2, width), bf16)] * 2,
            (place, tables, own, below, above, *far, norm_gain),
            [smem] + [vmem] * 7,
            flops=4 * slots * tok_dev * width,
        )

    def assembled(blocks, pieces):
        return call(
            functools.partial(assemble, pieces),
            "assemble",
            [((slots, width), bf16)],
            blocks,
            [anywhere] * len(blocks),
            [pltpu.SemaphoreType.DMA((len(pieces),))],
            out_specs=[anywhere],
        )[0]

    far_f = far_along_z(below_f, above_f)
    tables, far_f = lax.optimization_barrier((tables, far_f))
    below_f, above_f, x_ring = lax.optimization_barrier((below_f, above_f, x_sel))
    below_b, above_b = along_z(x_ring)
    near_f, other_f = picked(0, x_fwd, below_f, above_f, far_f)
    other_f = move(other_f, 0, 1)
    send_d = call(
        bind(weigh_rows),
        "weigh_rows",
        [((2 * capacity, width), bf16)] * 4,
        (place, tables, cot, pair_cot, head),
        [smem] + [vmem] * 4,
        flops=8 * slots * tok_dev * width,
    )
    below_b, above_b, send_d = lax.optimization_barrier((below_b, above_b, send_d))
    far_b = far_along_z(below_b, above_b)
    near_b, other_b = picked(2, x_sel, below_b, above_b, far_b)
    other_b, send_d = lax.optimization_barrier((other_b, send_d))
    other_b = move(other_b, 0, 1)
    got_d = [move(send_d[step % 4], step, 0) if step else send_d[0] for step in (0, 1, 3, 2)]

    halves = [(0, 0, slots // 2, 0), (1, 0, slots // 2, slots // 2)]
    quarters = [
        (at, side * capacity, capacity, (side * 4 + at) * capacity)
        for side in range(2)
        for at in range(4)
    ]
    rows_f = assembled((near_f, other_f), halves)
    gate_pre = jnp.dot(rows_f, wg, preferred_element_type=f32)
    up_pre = jnp.dot(rows_f, wu, preferred_element_type=f32)
    hidden_f = lax.optimization_barrier((jax.nn.silu(gate_pre) * up_pre).astype(bf16))
    out_f = jnp.dot(hidden_f, wd, preferred_element_type=f32).astype(bf16)
    ret_send, dots = call(
        bind(attach_dots),
        "attach_dots",
        [((groups, capacity, width + extra), bf16), ((groups, 1, capacity), f32)],
        (place, out_f, head),
        [smem, vmem, vmem],
    )
    dots = exchange(dots)
    last_block = pl.BlockSpec((slots, extra), lambda i: (0, width // extra))
    coef, ret_send = call(
        bind(find_coefs),
        "find_coefs",
        [((tok_dev, 1), f32), ((slots, width + extra), bf16)],
        (
            place,
            table,
            x_fwd,
            head,
            verdict_labels[:, None],
            dots,
            ret_send.reshape(slots, width + extra),
        ),
        [smem] + [vmem] * 5 + [last_block],
        out_specs=[vmem, last_block],
        aliases={6: 1},
    )
    got_d, other_b, ret_send = lax.optimization_barrier((got_d, other_b, ret_send))
    ret_f = exchange(ret_send.reshape(groups, capacity, width + extra))
    ret_f = ret_f.reshape(slots, width + extra)
    rows_b = assembled((near_b, other_b), halves)
    rows_d = assembled(tuple(got_d), quarters)

    gate_pre = jnp.dot(rows_b, wg, preferred_element_type=f32)
    up_pre = jnp.dot(rows_b, wu, preferred_element_type=f32)
    sig = jax.nn.sigmoid(gate_pre)
    silu = gate_pre * sig
    hidden_b = (silu * up_pre).astype(bf16)
    d_hidden = contract_cols(rows_d, wd)
    d_gate = (d_hidden * up_pre * sig * (1.0 + gate_pre * (1.0 - sig))).astype(bf16)
    d_up = (d_hidden * silu).astype(bf16)
    d_rows = (contract_cols(d_gate, wg) + contract_cols(d_up, wu)).astype(bf16)

    (d_rows,) = call(
        bind(split_rows),
        "split_rows",
        [((groups, capacity, width), bf16)],
        (place, d_rows),
        [smem, vmem],
    )
    ret_f, d_rows = lax.optimization_barrier((ret_f, d_rows))
    ret_d = exchange(d_rows).reshape(slots, width)
    (layer_out,) = call(
        bind(join_forward),
        "join_forward",
        [((tok_dev, width), bf16)],
        (table, ret_f, x_fwd),
        [vmem] * 3,
    )
    next_input = passed_along(layer_out, "section", 1)
    coef_rows = jnp.sum(ret_f[:, width:].astype(f32), axis=1).reshape(groups, capacity)
    coef_rows = jnp.take(coef_rows, order, axis=0).reshape(slots, 1)

    def scaled(value):
        return (value.astype(f32) * coef_rows).astype(bf16)

    grad_d = contract_rows(scaled(hidden_b), rows_d).astype(bf16)
    grad_g = contract_rows(rows_b, scaled(d_gate)).astype(bf16)
    grad_u = contract_rows(rows_b, scaled(d_up)).astype(bf16)

    ret_d, grad_d, grad_g, grad_u = lax.optimization_barrier((ret_d, grad_d, grad_g, grad_u))
    d_input, gain_local = call(
        bind(join_backward),
        "join_backward",
        [((tok_dev, width), bf16), ((1, width), f32)],
        (place, table, ret_d, x_sel, cot, coef, norm_gain, head),
        [smem] + [vmem] * 7,
        [pltpu.VMEM((tok_dev, width), f32)],
    )
    prev_grad = passed_along(d_input, "section", -1)
    (next_input,) = call(
        copy_rows, "copy_rows", [((tok_dev, width), bf16)], (next_input, gain_local), [vmem] * 2
    )
    gain_grad = gain_local
    step = groups // 2
    while step:
        gain_grad = gain_grad + lax.ppermute(
            gain_grad, "expert", [(source, source ^ step) for source in range(groups)]
        )
        step //= 2
    return (
        next_input[None],
        prev_grad[None],
        gain_grad,
        grad_g[None, None],
        grad_u[None, None],
        grad_d[None, None],
    )


def solution(mesh):
    return jax.shard_map(
        on_device,
        mesh=mesh,
        in_specs=(
            P("section", "expert", None),
            P("section", "expert", None),
            P("section", "expert", None),
            P("section", "expert", None),
            P("section", "expert", None),
            P("section", "expert", None),
            P("section", "expert", None),
            P("section", "expert", None, None),
            P("section", "expert", None, None),
            P("section", "expert", None, None),
            P("section", None),
            P(),
            P("expert"),
        ),
        out_specs=(
            P("section", "expert", None),
            P("section", "expert", None),
            P("section", None),
            P("section", "expert", None, None),
            P("section", "expert", None, None),
            P("section", "expert", None, None),
        ),
        check_vma=False,
    )
```
